32 devices in a mesh: band: 4 (over y, x), col: 8 (over z, core).
Axes of the slice: x: 2, y: 2, z: 4, core: 2. Of those that a mesh axis runs over, the one named last changes fastest.
Arguments:
- control: bfloat16 [4, 640, 320, 137], P('band', 'col'), may hold values from -6 to 6
- vertical_root: bfloat16 [3, 137, 128], replicated, may hold values from -0.5 to 0.5
- legendre: bfloat16 [320, 320, 320], P('col'), may hold values from -0.3125 to 0.3125
- band_filter: float32 [3, 320], replicated, may hold values from 0.3 to 1.7
- row_plan: int32 [4, 2], P('band'), may hold values from 0 to 16, as said below
- wave_order: int32 [320], replicated, may hold values from 0 to 319, each once
- lat_points: int32 [320], P('col'), may hold values from 16 to 640, as said below
- support: int32 [3, 2], replicated, may hold values from 0 to 320, as said below
Outputs:
- spectrum: float32 [320, 320, 2, 128], P('col', 'band')
The draws below stay inside these ranges and needn't reach their ends.
Inputs may be any that keep to these rules, and one draw needn't show every extreme that they name: `row_plan`: column 0 is the band of the row: 2 (coarsest) on max(1, 0) rows, 1 on max(1, 0) rows, 0 (finest) on the rest, rows drawn at random. Column 1 is the row's first output level; some row starts at 0 and some at 16. `lat_points`: counts rise with the distance from the nearest pole, apart from a jitter of up to 7 points between neighbouring latitudes; latitudes near the equator have all 640 points. `support`: row b is band b; band 0 ends at 320, band 2 starts at 0; every band's range is non-empty and the ranges of neighbouring bands intersect.
All inputs are finite; a program needn't handle non-finite values.
Results may differ from the reference program's by a relative error of at most 0.012.
Values may be sent and summed in bfloat16 or wider, within the bound.
A program may use at most 128 MiB of HBM per device.

```python
import math
import jax
import jax.numpy as jnp
from jax import lax

LON = 640
LAT = 320
M = 320
N = 320
LEV = 137
LVR = 112
SHIFT = 16
LEVW = 128
N_BAND = 4


def draw_row_plan(key, part):
    key_perm, key_start = jax.random.split(jax.random.fold_in(key, 11), 2)
    coarse = max(1, N_BAND // 16)
    middle = max(1, 3 * N_BAND // 16)
    shuffled = jax.random.permutation(key_perm, N_BAND)
    position = jnp.argsort(shuffled).astype(jnp.int32)
    band_column = jnp.where(position < coarse, 2, jnp.where(position < coarse + middle, 1, 0)).astype(jnp.int32)
    first_level = jax.random.randint(key_start, (N_BAND,), 0, SHIFT + 1, dtype=jnp.int32)
    first_level = jnp.where(position == 0, SHIFT, jnp.where(position == N_BAND - 1, 0, first_level)).astype(jnp.int32)
    return jnp.stack([band_column, first_level], axis=1).astype(jnp.int32)


def draw_lat_points(key, part):
    lat_axis = jnp.arange(LAT, dtype=jnp.int32)
    pole_dist = jnp.minimum(lat_axis, LAT - 1 - lat_axis)
    jitter = jax.random.randint(jax.random.fold_in(key, 23), (LAT,), 0, 8, dtype=jnp.int32)
    counts = 16 + 3 * LON * pole_dist // LAT + jitter
    return jnp.minimum(counts, LON).astype(jnp.int32)


def draw_support(key, part):
    keys = jax.random.split(jax.random.fold_in(key, 37), 4)
    fine_lo = jax.random.randint(keys[0], (), N // 8, N // 4 + 1, dtype=jnp.int32)
    mid_lo = jax.random.randint(keys[1], (), N // 16, N // 8 + 1, dtype=jnp.int32)
    mid_hi = jax.random.randint(keys[2], (), N // 2, 3 * N // 4 + 1, dtype=jnp.int32)
    coarse_hi = jax.random.randint(keys[3], (), N // 4, N // 2 + 1, dtype=jnp.int32)
    lows = jnp.stack([fine_lo, mid_lo, jnp.zeros((), jnp.int32)])
    highs = jnp.stack([jnp.full((), N, jnp.int32), mid_hi, coarse_hi])
    return jnp.stack([lows, highs], axis=1).astype(jnp.int32)


def levels(own_key, extent, shards, low, top_value):
    def one(dim, shards_of):
        draws = jax.random.uniform(jax.random.fold_in(jax.random.fold_in(own_key, 6), dim), (shards_of,), jnp.float32, low / len(shards), top_value / len(shards))
        return jnp.repeat(jnp.exp(draws), extent[dim] // shards_of).reshape((-1,) + (1,) * (len(extent) - dim - 1))

    factor_of = one(*shards[0])
    for cut in shards[1:]:
        factor_of = factor_of * one(*cut)
    return factor_of


def noise(own_key, extent, scale, limit, shards=(), held_as=jnp.bfloat16):
    factor_of = levels(own_key, extent, shards, -0.22, 0.18) if shards else 1.0
    entries = jax.random.normal(own_key, extent, jnp.float32) * scale * factor_of
    return jnp.minimum(jnp.maximum(entries, -limit), limit).astype(held_as)


def setup_inputs(seed: int = 0) -> dict:
    seeds = jax.random.split(jax.random.key(seed), 9)
    control = noise(seeds[0], (N_BAND, LON, LAT, LEV), 1.0, 6.0, ((0, 4), (1, 8)))
    vertical_root = noise(seeds[1], (3, LEV, LEVW), LEV ** -0.5, 0.5)
    legendre = noise(seeds[2], (M, LAT, N), LAT ** -0.5, 0.3125, ((0, 8),))
    band_filter = jnp.clip(jax.random.uniform(seeds[3], (3, N), jnp.float32, 0.3, 1.7), 0.3, 1.7)
    row_plan = draw_row_plan(jax.random.fold_in(seeds[8], 71), 0)
    wave_order = jax.random.permutation(seeds[5], M).astype(jnp.int32)
    lat_points = draw_lat_points(jax.random.fold_in(seeds[8], 71), 0)
    support = draw_support(jax.random.fold_in(seeds[8], 71), 0)
    return dict(control=control, vertical_root=vertical_root, legendre=legendre, band_filter=band_filter, row_plan=row_plan, wave_order=wave_order, lat_points=lat_points, support=support)


def dft_rows(points, wave_list, lon_count):
    lon_index = jnp.arange(lon_count, dtype=jnp.int32)[:, None]
    phase_step = wave_list[None, :] * lon_index % points
    angles = 2.0 * math.pi * phase_step.astype(jnp.float32) / points.astype(jnp.float32)
    live_mask = (lon_index < points).astype(jnp.float32) / jnp.sqrt(points.astype(jnp.float32))
    return (jnp.concatenate([jnp.cos(angles), -jnp.sin(angles)], axis=1) * live_mask).astype(jnp.bfloat16)

def reference(control, vertical_root, legendre, band_filter, row_plan, wave_order, lat_points, support):
    row_count, lon_count, lat_count, lev_count = control.shape
    mode_count = legendre.shape[0]
    degree_count = legendre.shape[2]
    degree = jnp.arange(degree_count, dtype=jnp.int32)
    triangle = (degree[None, :] >= wave_order[:, None]).astype(jnp.float32)
    legendre_f = legendre.astype(jnp.float32)

    def one_row(running, row_index):
        band_id = row_plan[row_index, 0]
        level_start = row_plan[row_index, 1]
        root_band = lax.dynamic_index_in_dim(vertical_root, band_id, 0, keepdims=False)
        root_block = lax.dynamic_slice_in_dim(root_band, level_start, LVR, 1)
        flat = lax.dynamic_index_in_dim(control, row_index, 0, keepdims=False).reshape(lon_count * lat_count, lev_count)
        grid_field = jnp.dot(flat, root_block, preferred_element_type=jnp.float32).astype(jnp.bfloat16)
        grid_field = grid_field.reshape(lon_count, lat_count, LVR)

        def one_lat(lat_index):
            weights = dft_rows(lat_points[lat_index], wave_order, lon_count)
            column = lax.dynamic_index_in_dim(grid_field, lat_index, 1, keepdims=False)
            return lax.dot_general(weights, column, (((0,), (0,)), ((), ())), preferred_element_type=jnp.float32).astype(jnp.bfloat16)
        fourier = lax.map(one_lat, jnp.arange(lat_count, dtype=jnp.int32)).reshape(lat_count, 2, mode_count, LVR)
        spectral = jnp.einsum('xpsl,sxn->snpl', fourier.astype(jnp.float32), legendre_f)
        bounds = lax.dynamic_index_in_dim(support, band_id, 0, keepdims=False)
        filter_row = lax.dynamic_index_in_dim(band_filter, band_id, 0, keepdims=False)
        window = filter_row * ((degree >= bounds[0]) & (degree < bounds[1])).astype(jnp.float32)
        contribution = (spectral * (triangle * window[None, :])[:, :, None, None]).astype(jnp.bfloat16)
        contribution = lax.optimization_barrier(contribution).astype(jnp.float32)
        placed = jnp.zeros((mode_count, degree_count, 2, LEVW), jnp.float32)
        placed = lax.dynamic_update_slice_in_dim(placed, contribution, level_start, 3)
        return (running + placed, None)
    initial = jnp.zeros((mode_count, degree_count, 2, LEVW), jnp.float32)
    summed, unused = lax.scan(one_row, initial, jnp.arange(row_count, dtype=jnp.int32))
    return summed
```

```python
import functools
import math

import jax
import jax.numpy as jnp
from jax import lax
from jax.experimental import pallas as pl
from jax.experimental.pallas import tpu as pltpu
from jax.sharding import PartitionSpec as P

LVR = 112
CHUNKS = (2, 2, 1)
LANES = 128
GROUP = 16
PACK = LVR // GROUP
MESH = pl.DeviceIdType.MESH


def sine(theta):
    square = theta * theta
    value = -1.0 / 39916800.0 * square + 1.0 / 362880.0
    value = value * square - 1.0 / 5040.0
    value = value * square + 1.0 / 120.0
    value = value * square - 1.0 / 6.0
    value = value * square + 1.0
    return value * theta


def weights_kernel(points_ref, wave_ref, *out_refs):
    count = jnp.full((1, 1), points_ref[pl.program_id(0)], jnp.int32).astype(jnp.float32)
    lons = out_refs[0].shape[2]
    lanes = 128
    lon = lax.broadcasted_iota(jnp.int32, (1, lons), 1).astype(jnp.float32)
    full = 4.0 * count
    inverse = 1.0 / full
    unit = (2.0 * math.pi) * inverse
    scale = jnp.where(lon < count, lax.rsqrt(count), 0.0)
    nearest = 1.5 * 2.0**23
    first = 0
    for out_ref in out_refs:
        half = out_ref.shape[1] // 2
        tile = 8 if half % 16 else 16

        def rows(k, carry, out_ref=out_ref, first=first, tile=tile, half=half):
            at = pl.multiple_of(k * tile, tile)
            turns = wave_ref[pl.ds(first + at, tile), :] * lon[:, :lanes]
            whole = (turns * inverse + nearest) - nearest
            rest = turns - whole * full
            cos = sine((count - jnp.abs(rest)) * unit)
            away = jnp.abs(rest - count)
            sin = sine((count - jnp.minimum(away, full - away)) * unit)
            middle = lanes // 2
            cos_half = jnp.broadcast_to(cos[:, middle : middle + 1], cos.shape)
            sin_half = jnp.broadcast_to(sin[:, middle : middle + 1], sin.shape)
            cos_step = cos_half * cos_half - sin_half * sin_half
            sin_step = 2.0 * (cos_half * sin_half)
            for lo in range(0, lons, lanes):
                if lo:
                    cos, sin = (
                        cos * cos_step - sin * sin_step,
                        sin * cos_step + cos * sin_step,
                    )
                part = scale[:, lo : lo + lanes]
                out_ref[0, pl.ds(at, tile), lo : lo + lanes] = (cos * part).astype(
                    jnp.bfloat16
                )
                out_ref[0, pl.ds(half + at, tile), lo : lo + lanes] = (-sin * part).astype(
                    jnp.bfloat16
                )
            return carry

        lax.fori_loop(0, half // tile, rows, 0)
        first += half


def dft_weights(points, chunks, lon_count):
    lats = points.shape[0]
    shapes = [(lats, 2 * waves.size, lon_count) for waves in chunks]
    wave = jnp.concatenate([waves.reshape(-1) for waves in chunks])
    wave = 4.0 * wave.astype(jnp.float32)[:, None]
    return pl.pallas_call(
        weights_kernel,
        grid_spec=pltpu.PrefetchScalarGridSpec(
            num_scalar_prefetch=1,
            grid=(lats,),
            in_specs=[pl.BlockSpec(wave.shape, lambda i, p: (0, 0))],
            out_specs=[pl.BlockSpec((1,) + sh[1:], lambda i, p: (i, 0, 0)) for sh in shapes],
        ),
        out_shape=[jax.ShapeDtypeStruct(sh, jnp.bfloat16) for sh in shapes],
        cost_estimate=pl.CostEstimate(
            flops=20 * lats * wave.shape[0] * lon_count,
            bytes_accessed=4 * lats * wave.shape[0] * lon_count,
            transcendentals=0,
        ),
        name="weights",
    )(points, wave)


def dft_kernel(weight_ref, grid_ref, out_ref):
    lons = grid_ref.shape[0] * grid_ref.shape[2]
    owners, _, parts, slots, levels = out_ref.shape
    half = owners * slots
    for i in range(grid_ref.shape[1]):
        column = grid_ref[:, i].reshape(lons, levels)
        result = jnp.dot(weight_ref[i], column, preferred_element_type=jnp.float32)
        for p in range(parts):
            piece = result[p * half : (p + 1) * half].reshape(owners, slots, levels)
            out_ref[:, i, p] = piece.astype(jnp.bfloat16)


def dft(weights, grid_field, owners):
    lats, cols, lons = weights.shape
    ranks, _, lon_local, levels = grid_field.shape
    slots = cols // (2 * owners)
    block = max(d for d in range(1, 9) if lats % d == 0)
    return pl.pallas_call(
        dft_kernel,
        grid=(lats // block,),
        in_specs=[
            pl.BlockSpec((block, cols, lons), lambda i: (i, 0, 0)),
            pl.BlockSpec((ranks, block, lon_local, levels), lambda i: (0, i, 0, 0)),
        ],
        out_specs=pl.BlockSpec((owners, block, 2, slots, levels), lambda i: (0, i, 0, 0, 0)),
        out_shape=jax.ShapeDtypeStruct((owners, lats, 2, slots, levels), jnp.bfloat16),
        cost_estimate=pl.CostEstimate(
            flops=2 * lats * cols * lons * levels,
            bytes_accessed=2 * lats * (cols * lons + (cols + lons) * levels),
            transcendentals=0,
        ),
        name="dft",
    )(weights, grid_field)


def per_device_plain(
    control, vertical_root, legendre, band_filter, row_plan, wave_order, lat_points, support
):
    owners = lax.axis_size("col")
    band_id = row_plan[0, 0]
    level_start = row_plan[0, 1]
    root_band = lax.dynamic_index_in_dim(vertical_root, band_id, 0, keepdims=False)
    level = jnp.arange(root_band.shape[1], dtype=jnp.int32)
    inside = (level >= level_start) & (level < level_start + LVR)
    root_block = jnp.where(inside[None, :], root_band, jnp.zeros_like(root_band))
    columns = control[0]
    lon_local, lat_count, _ = columns.shape
    rooted = jnp.einsum(
        "jik,kl->ijl", columns, root_block, preferred_element_type=jnp.float32
    ).astype(jnp.bfloat16)
    rooted = rooted.reshape(owners, lat_count // owners, lon_local, -1)
    grid_field = lax.all_to_all(rooted, "col", split_axis=0, concat_axis=0, tiled=True)
    lon_count = lon_local * owners
    lat_local = lat_count // owners

    slot_count = legendre.shape[0]
    degree_count = legendre.shape[2]
    ends = [slot_count * sum(CHUNKS[: c + 1]) // sum(CHUNKS) for c in range(len(CHUNKS))]
    spans = list(zip([0] + ends[:-1], ends))
    waves = wave_order.reshape(owners, slot_count)
    owned_waves = lax.dynamic_index_in_dim(waves, lax.axis_index("col"), 0, keepdims=False)
    degree = jnp.arange(degree_count, dtype=jnp.int32)
    bounds = lax.dynamic_index_in_dim(support, band_id, 0, keepdims=False)
    filter_row = lax.dynamic_index_in_dim(band_filter, band_id, 0, keepdims=False)
    window = filter_row * ((degree >= bounds[0]) & (degree < bounds[1])).astype(jnp.float32)

    weights = dft_weights(lat_points, [waves[:, lo:hi] for lo, hi in spans], lon_count)
    outputs = []
    fourier = dft(weights[0], grid_field, owners)
    for c, (lo, hi) in enumerate(spans):
        owned = lax.all_to_all(fourier, "col", split_axis=0, concat_axis=0, tiled=True)
        if c + 1 < len(spans):
            fourier = dft(weights[c + 1], grid_field, owners)
        if c:
            fourier, owned, _ = lax.optimization_barrier((fourier, owned, contribution))
        else:
            fourier, owned = lax.optimization_barrier((fourier, owned))
        owned = owned.reshape(lat_count, 2, hi - lo, owned.shape[4])
        spectral = jnp.einsum(
            "xpsl,sxn->snpl",
            owned,
            legendre[lo:hi],
            preferred_element_type=jnp.float32,
        )
        spectral_weight = (degree[None, :] >= owned_waves[lo:hi][:, None]).astype(
            jnp.float32
        ) * window[None, :]
        contribution = (spectral * spectral_weight[:, :, None, None]).astype(jnp.bfloat16)
        if c:
            contribution, outputs[-1] = lax.optimization_barrier((contribution, outputs[-1]))
        outputs.append(
            lax.psum_scatter(contribution, "band", scatter_dimension=1, tiled=True)
        )
    return jnp.concatenate(outputs, axis=0).astype(jnp.float32)


def greet(axes):
    barrier = pltpu.get_barrier_semaphore()
    total = 0
    for axis in axes:
        size, me = lax.axis_size(axis), lax.axis_index(axis)
        for d in range(1, size):
            pl.semaphore_signal(
                barrier,
                inc=1,
                device_id={axis: lax.rem(me + d, size)},
                device_id_type=MESH,
            )
        total += size - 1
    pl.semaphore_wait(barrier, total)


def lat_weights(count, wave_ref, lons, out_ref, index, tile):
    full = 4.0 * count
    inverse = 1.0 / full
    unit = (2.0 * math.pi) * inverse
    lon = lax.broadcasted_iota(jnp.int32, (1, lons), 1).astype(jnp.float32)
    scale = jnp.where(lon < count, lax.rsqrt(count), 0.0)
    nearest = 1.5 * 2.0**23
    half = wave_ref.shape[0]

    def rows(k, carry):
        at = pl.multiple_of(k * tile, tile)
        turns = wave_ref[pl.ds(at, tile), :] * lon[:, :LANES]
        whole = (turns * inverse + nearest) - nearest
        rest = turns - whole * full
        cos = sine((count - jnp.abs(rest)) * unit)
        away = jnp.abs(rest - count)
        sin = sine((jnp.minimum(away, full - away) - count) * unit)
        middle = LANES // 2
        cos_half = jnp.broadcast_to(cos[:, middle : middle + 1], cos.shape)
        sin_half = jnp.broadcast_to(sin[:, middle : middle + 1], sin.shape)
        cos_step = cos_half * cos_half - sin_half * sin_half
        sin_step = 2.0 * (cos_half * sin_half)
        for lo in range(0, lons, LANES):
            if lo:
                cos, sin = (
                    cos * cos_step - sin * sin_step,
                    sin * cos_step + cos * sin_step,
                )
            part = scale[:, lo : lo + LANES]
            out_ref[index, pl.ds(at, tile), lo : lo + LANES] = (cos * part).astype(
                jnp.bfloat16
            )
            out_ref[index, pl.ds(half + at, tile), lo : lo + LANES] = (
                sin * part
            ).astype(jnp.bfloat16)
        return carry

    lax.fori_loop(0, half // tile, rows, 0)


def exchange(src, dst, send_sem, recv_sem, k, d, axis="col"):
    size, me = lax.axis_size(axis), lax.axis_index(axis)
    to = lax.rem(me + d, size)
    return pltpu.make_async_remote_copy(
        src_ref=src.at[k, to],
        dst_ref=dst.at[k, me],
        send_sem=send_sem.at[k, d],
        recv_sem=recv_sem.at[k, d],
        device_id={axis: to},
        device_id_type=MESH,
    )


def front_kernel(
    points_ref,
    control_ref,
    root_ref,
    rel_ref,
    wave_ref,
    out_ref,
    ctl,
    rooted,
    sent,
    got,
    weight,
    turned,
    packed,
    ctl_sem,
    send_sem,
    recv_sem,
    own_sem,
    out_sem,
):
    chunks, owners, _, lon_local, _ = sent.shape
    blocks = ctl.shape[0]
    lons = owners * lon_local
    waves = wave_ref.shape[0]
    me = lax.axis_index("col")
    spare = rel_ref[0:1, :] >= LVR

    def load(block):
        at = pl.multiple_of(16 * block, 16)
        return pltpu.make_async_copy(
            control_ref.at[:, pl.ds(at, 16), :], ctl.at[block], ctl_sem.at[block]
        )

    def own(k):
        return pltpu.make_async_copy(sent.at[k, me], got.at[k, me], own_sem.at[k])

    def send(k):
        for d in range(1, owners):
            exchange(sent, got, send_sem, recv_sem, k, d).start()
        own(k).start()

    order = sorted(range(chunks), key=lambda o: (min((2 * o) % chunks, (2 * o + 1) % chunks), o))
    pairs = blocks // chunks

    def load_all(o):
        def one(b, carry):
            load(chunks * b + o).start()
            return carry

        lax.fori_loop(0, pairs, one, 0)

    for o in order:
        load_all(o)
    greet(["col"])

    filled = [0] * chunks
    next_chunk = 0
    for o in order:

        def root(b, carry, o=o):
            block = chunks * b + o
            load(block).wait()
            lhs = ctl[block].reshape(lon_local * 16, ctl.shape[3])
            rooted[...] = jnp.dot(lhs, root_ref[...], preferred_element_type=jnp.float32)
            for h in range(2):
                q = 2 * o + h
                to, k = 2 * b + q // chunks, q % chunks
                last = rooted[pl.ds(8 * h + PACK, lon_local, stride=16), :]
                for g in range(PACK):
                    mine = rooted[pl.ds(8 * h + g, lon_local, stride=16), :]
                    moved = pltpu.roll(last, LVR - GROUP * g, 1)
                    sent[k, to, g] = jnp.where(spare, moved, mine).astype(jnp.bfloat16)
            return carry

        lax.fori_loop(0, pairs, root, 0)
        for h in range(2):
            filled[(2 * o + h) % chunks] += 1
        while next_chunk < min(2, chunks) and filled[next_chunk] == 2:
            send(next_chunk)
            next_chunk += 1

    eighth = waves // 8
    groups = eighth // owners

    def transform(lat, x):
        for p in range(2):
            res = jnp.dot(
                weight[lat, p * waves : (p + 1) * waves, :],
                x,
                preferred_element_type=jnp.float32,
            )
            last = res[PACK * eighth :]
            for g in range(PACK):
                moved = pltpu.roll(last, LVR - GROUP * g, 1)
                piece = jnp.where(spare, moved, res[g * eighth : (g + 1) * eighth])
                turned[pl.ds(g * eighth * 16 + p * 8 + lat, eighth, stride=16), :] = piece

    def out_copy(k):
        return pltpu.make_async_copy(
            packed.at[lax.rem(k, 2)], out_ref.at[:, :, k], out_sem.at[k]
        )

    def chunk(k, carry):
        def make(lat, c):
            count = jnp.full((1, 1), points_ref[8 * k + lat], jnp.int32).astype(jnp.float32)
            lat_weights(count, wave_ref, lons, weight, lat, 32 if waves % 32 == 0 else 16)
            return c

        lax.fori_loop(0, 8, make, 0)
        for d in range(1, owners):
            exchange(sent, got, send_sem, recv_sem, k, d).wait()
        own(k).wait()

        @pl.when(k + 2 < chunks)
        def _():
            send(k + 2)

        def plain(g, c):
            transform(g, got[k, :, g].reshape(lons, LANES))
            return c

        lax.fori_loop(0, PACK, plain, 0)
        rel = rel_ref[0:1, :]
        x = jnp.zeros((lons, LANES), jnp.float32)
        for g in range(PACK):
            moved = got[k, :, g].reshape(lons, LANES).astype(jnp.float32)
            moved = pltpu.roll(moved, LANES - LVR + GROUP * g, 1)
            here = (rel >= GROUP * g) & (rel < GROUP * (g + 1))
            x = jnp.where(here, moved, x)
        transform(PACK, x.astype(jnp.bfloat16))

        @pl.when(k >= 2)
        def _():
            out_copy(k - 2).wait()

        slot = lax.rem(k, 2)
        for g in range(PACK):
            for c in range(groups):
                at = (g * eighth + c * owners) * 16
                rows = turned[at : at + 16 * owners, :].reshape(owners, 16, LANES)
                packed[slot, c, :, g] = rows.astype(jnp.bfloat16)
        out_copy(k).start()
        return carry

    lax.fori_loop(0, chunks, chunk, 0)
    for k in range(max(0, chunks - 2), chunks):
        out_copy(k).wait()


def front(points, control, root, rel, wave, owners):
    lon_local, lats, levels = control.shape
    chunks = lats // owners // 8
    waves = wave.shape[0]
    groups = waves // 8 // owners
    lons = owners * lon_local
    blocks = lats // 16
    bf16 = jnp.bfloat16
    any_spec = pl.BlockSpec(memory_space=pl.ANY)
    vmem_spec = pl.BlockSpec(memory_space=pltpu.VMEM)
    return pl.pallas_call(
        front_kernel,
        in_specs=[
            pl.BlockSpec(memory_space=pltpu.SMEM),
            any_spec,
            vmem_spec,
            vmem_spec,
            vmem_spec,
        ],
        out_specs=any_spec,
        out_shape=jax.ShapeDtypeStruct((groups, owners, chunks, PACK, 16, LANES), bf16),
        scratch_shapes=[
            pltpu.VMEM((blocks, lon_local, 16, levels), bf16),
            pltpu.VMEM((lon_local * 16, LANES), jnp.float32),
            pltpu.VMEM((chunks, owners, PACK, lon_local, LANES), bf16),
            pltpu.VMEM((chunks, owners, PACK, lon_local, LANES), bf16),
            pltpu.VMEM((8, 2 * waves, lons), bf16),
            pltpu.VMEM((PACK * waves // 8 * 16, LANES), jnp.float32),
            pltpu.VMEM((2, groups, owners, PACK, 16, LANES), bf16),
            pltpu.SemaphoreType.DMA((blocks,)),
            pltpu.SemaphoreType.DMA((chunks, owners)),
            pltpu.SemaphoreType.DMA((chunks, owners)),
            pltpu.SemaphoreType.DMA((chunks,)),
            pltpu.SemaphoreType.DMA((chunks,)),
        ],
        compiler_params=pltpu.CompilerParams(
            collective_id=0, has_side_effects=True, vmem_limit_bytes=56 * 2**20
        ),
        name="front",
    )(points, control, root, rel, wave)


def back_kernel(
    fourier_ref,
    legendre_ref,
    slot_ref,
    window_ref,
    rel_ref,
    out_ref,
    got,
    leg,
    leg_t,
    last,
    part,
    other,
    summed,
    send_sem,
    recv_sem,
    own_sem,
    leg_sem,
    part_sem,
    other_sem,
    out_sem,
):
    groups, owners, chunks = got.shape[:3]
    bands, _, _, degrees, _ = part.shape[1:]
    lats = owners * chunks * 8
    total = leg.shape[3]
    me = lax.axis_index("col")
    band = lax.axis_index("band")
    quarter = 8 // 2

    def own(c):
        return pltpu.make_async_copy(fourier_ref.at[c, me], got.at[c, me], own_sem.at[c])

    def send(c):
        for d in range(1, owners):
            exchange(fourier_ref, got, send_sem, recv_sem, c, d).start()
        own(c).start()

    def load(c):
        at = pl.multiple_of(8 * c, 8)
        return pltpu.make_async_copy(
            legendre_ref.at[pl.ds(at, 8)], leg.at[lax.rem(c, 2)], leg_sem.at[c]
        )

    def give(c, h, d):
        to = lax.rem(band + d, bands)
        return pltpu.make_async_remote_copy(
            src_ref=part.at[lax.rem(c, 2), to, pl.ds(quarter * h, quarter)],
            dst_ref=other.at[d - 1, c, pl.ds(quarter * h, quarter)],
            send_sem=part_sem.at[c, h, d],
            recv_sem=other_sem.at[c, h, d],
            device_id={"band": to},
            device_id_type=MESH,
        )

    def out_copy(c):
        at = pl.multiple_of(8 * c, 8)
        return pltpu.make_async_copy(
            summed.at[lax.rem(c, 2)], out_ref.at[pl.ds(at, 8)], out_sem.at[c]
        )

    def finish(c, h):
        for d in range(1, bands):
            give(c, h, d).wait_recv()
        slot = lax.rem(c, 2)
        for sl in range(quarter * h, quarter * (h + 1)):
            for p in range(2):
                acc = part[slot, band, sl, p].astype(jnp.float32)
                for d in range(1, bands):
                    acc = acc + other[d - 1, c, sl, p].astype(jnp.float32)
                summed[slot, sl, pl.ds(p, degrees, stride=2), :] = acc

    load(0).start()
    if groups > 1:
        load(1).start()
    greet(["col", "band"])
    for c in range(min(2, groups)):
        send(c)
    rel = rel_ref[0:1, :]
    degree = lax.broadcasted_iota(jnp.int32, (total, LANES), 0).astype(jnp.float32)

    def slot_out(c, sl, halves):
        res = lax.dot_general(
            leg_t[sl],
            jnp.concatenate([h.astype(jnp.bfloat16) for h in halves], axis=1),
            (((1,), (0,)), ((), ())),
            preferred_element_type=jnp.float32,
        )
        keep = jnp.where(degree >= slot_ref[8 * c + sl], window_ref[...], 0.0)
        for p in range(2):
            value = (res[:, p * LANES : (p + 1) * LANES] * keep).astype(jnp.bfloat16)
            part[lax.rem(c, 2), :, sl, p] = value.reshape(bands, degrees, LANES)

    def group(c, carry):
        load(c).wait()
        slot = lax.rem(c, 2)
        for sl in range(8):
            leg_t[sl] = leg[slot, sl].T

        @pl.when(c + 2 < groups)
        def _():
            load(c + 2).start()

        for d in range(1, owners):
            exchange(fourier_ref, got, send_sem, recv_sem, c, d).wait()
        own(c).wait()

        @pl.when(c + 2 < groups)
        def _():
            send(c + 2)

        @pl.when(c >= 2)
        def _():
            for h in range(2):
                for d in range(1, bands):
                    give(c - 2, h, d).wait_send()

        for sl in range(PACK):
            value = got[c, :, :, sl].astype(jnp.float32).reshape(lats // 8, 2, 8, LANES)
            halves = [value[:, p].reshape(lats, LANES) for p in range(2)]
            here = (rel >= GROUP * sl) & (rel < GROUP * (sl + 1))
            for p in range(2):
                moved = pltpu.roll(halves[p], LANES - LVR + GROUP * sl, 1)
                before = last[p] if sl else jnp.zeros((lats, LANES), jnp.float32)
                last[p] = jnp.where(here, moved, before)
            slot_out(c, sl, halves)
            if sl == quarter - 1:
                for d in range(1, bands):
                    give(c, 0, d).start()
        slot_out(c, PACK, [last[0], last[1]])
        for d in range(1, bands):
            give(c, 1, d).start()

        @pl.when(c >= 3)
        def _():
            out_copy(c - 3).wait()

        @pl.when(c >= 1)
        def _():
            for h in range(2):
                finish(c - 1, h)
            out_copy(c - 1).start()

        return carry

    lax.fori_loop(0, groups, group, 0)
    if groups >= 3:
        out_copy(groups - 3).wait()
    for h in range(2):
        finish(groups - 1, h)
    out_copy(groups - 1).start()
    for c in range(max(0, groups - 2), groups):
        for h in range(2):
            for d in range(1, bands):
                give(c, h, d).wait_send()
        out_copy(c).wait()


def back(fourier, legendre, slots, window, rel, bands):
    groups, owners, chunks = fourier.shape[:3]
    slot_count, lats, total = legendre.shape
    degrees = total // bands
    bf16 = jnp.bfloat16
    any_spec = pl.BlockSpec(memory_space=pl.ANY)
    vmem_spec = pl.BlockSpec(memory_space=pltpu.VMEM)
    return pl.pallas_call(
        back_kernel,
        in_specs=[any_spec, any_spec, vmem_spec, vmem_spec, vmem_spec],
        out_specs=any_spec,
        out_shape=jax.ShapeDtypeStruct((slot_count, 2 * degrees, LANES), jnp.float32),
        scratch_shapes=[
            pltpu.VMEM((groups, owners, chunks, PACK, 16, LANES), bf16),
            pltpu.VMEM((2, 8, lats, total), bf16),
            pltpu.VMEM((8, total, lats), bf16),
            pltpu.VMEM((2, lats, LANES), jnp.float32),
            pltpu.VMEM((2, bands, 8, 2, degrees, LANES), bf16),
            pltpu.VMEM((bands - 1, groups, 8, 2, degrees, LANES), bf16),
            pltpu.VMEM((2, 8, 2 * degrees, LANES), jnp.float32),
            pltpu.SemaphoreType.DMA((groups, owners)),
            pltpu.SemaphoreType.DMA((groups, owners)),
            pltpu.SemaphoreType.DMA((groups,)),
            pltpu.SemaphoreType.DMA((groups,)),
            pltpu.SemaphoreType.DMA((groups, 2, bands)),
            pltpu.SemaphoreType.DMA((groups, 2, bands)),
            pltpu.SemaphoreType.DMA((groups,)),
        ],
        compiler_params=pltpu.CompilerParams(
            collective_id=1, has_side_effects=True, vmem_limit_bytes=56 * 2**20
        ),
        name="back",
    )(fourier, legendre, slots, window, rel)


def per_device_fused(
    control, vertical_root, legendre, band_filter, row_plan, wave_order, lat_points, support
):
    owners, bands = lax.axis_size("col"), lax.axis_size("band")
    slot_count, _, total = legendre.shape
    band_id, first = row_plan[0, 0], row_plan[0, 1]
    root = lax.dynamic_index_in_dim(vertical_root, band_id, 0, keepdims=False)
    bounds = lax.dynamic_index_in_dim(support, band_id, 0, keepdims=False)
    filter_row = lax.dynamic_index_in_dim(band_filter, band_id, 0, keepdims=False)
    rel = lax.rem(jnp.arange(LANES, dtype=jnp.int32) - first + LANES, LANES)
    degree = jnp.arange(total, dtype=jnp.int32)
    window = filter_row * ((degree >= bounds[0]) & (degree < bounds[1])).astype(jnp.float32)
    window = window[:, None] * (rel < LVR).astype(jnp.float32)[None, :]
    rel = jnp.broadcast_to(rel[None, :], (8, LANES))
    wave = wave_order.astype(jnp.float32)
    rows = wave.reshape(owners, slot_count // 8, 8).transpose(2, 1, 0).reshape(-1)
    rows = jnp.broadcast_to(4.0 * rows[:, None], (rows.shape[0], LANES))
    owned = lax.dynamic_index_in_dim(
        wave.reshape(owners, slot_count), lax.axis_index("col"), 0, keepdims=False
    )
    owned = jnp.broadcast_to(owned[:, None, None], (slot_count, 1, LANES))
    fourier = front(lat_points, control[0], root, rel, rows, owners)
    result = back(fourier, legendre, owned, window, rel, bands)
    return result.reshape(slot_count, total // bands, 2, LANES)


def per_device(control, vertical_root, legendre, *rest):
    owners, bands = lax.axis_size("col"), lax.axis_size("band")
    _, lon_local, lats, _ = control.shape
    slot_count, _, total = legendre.shape
    chunks = lats // owners // 8
    fits = (
        vertical_root.shape[2] == LANES
        and lats % (16 * owners // math.gcd(owners, 2)) == 0
        and lats % (8 * owners) == 0
        and owners % 2 == 0
        and chunks % 2 == 1
        and lon_local % 16 == 0
        and (owners * lon_local) % LANES == 0
        and slot_count % 8 == 0
        and (slot_count // 8 * owners) % 8 == 0
        and total % bands == 0
        and (total // bands) % 16 == 0
        and bands > 1
    )
    body = per_device_fused if fits else per_device_plain
    return body(control, vertical_root, legendre, *rest)


def solution(mesh):
    in_specs = (
        P("band", "col", None, None),
        P(),
        P("col", None, None),
        P(),
        P("band", None),
        P(),
        P("col"),
        P(),
    )
    out_specs = P("col", "band", None, None)
    return jax.shard_map(
        per_device, mesh=mesh, in_specs=in_specs, out_specs=out_specs, check_vma=False
    )
```

```python
import functools
import math

import jax
import jax.numpy as jnp
from jax import lax
from jax.experimental import pallas as pl
from jax.experimental.pallas import tpu as pltpu
from jax.sharding import PartitionSpec as P

LVR = 112
CHUNKS = (2, 2, 1)
LANES = 128
GROUP = 16
PACK = LVR // GROUP
MESH = pl.DeviceIdType.MESH


def sine(theta):
    square = theta * theta
    value = -1.0 / 39916800.0 * square + 1.0 / 362880.0
    value = value * square - 1.0 / 5040.0
    value = value * square + 1.0 / 120.0
    value = value * square - 1.0 / 6.0
    value = value * square + 1.0
    return value * theta


def weights_kernel(points_ref, wave_ref, *out_refs):
    count = jnp.full((1, 1), points_ref[pl.program_id(0)], jnp.int32).astype(jnp.float32)
    lons = out_refs[0].shape[2]
    lanes = 128
    lon = lax.broadcasted_iota(jnp.int32, (1, lons), 1).astype(jnp.float32)
    full = 4.0 * count
    inverse = 1.0 / full
    unit = (2.0 * math.pi) * inverse
    scale = jnp.where(lon < count, lax.rsqrt(count), 0.0)
    nearest = 1.5 * 2.0**23
    first = 0
    for out_ref in out_refs:
        half = out_ref.shape[1] // 2
        tile = 8 if half % 16 else 16

        def rows(k, carry, out_ref=out_ref, first=first, tile=tile, half=half):
            at = pl.multiple_of(k * tile, tile)
            turns = wave_ref[pl.ds(first + at, tile), :] * lon[:, :lanes]
            whole = (turns * inverse + nearest) - nearest
            rest = turns - whole * full
            cos = sine((count - jnp.abs(rest)) * unit)
            away = jnp.abs(rest - count)
            sin = sine((count - jnp.minimum(away, full - away)) * unit)
            middle = lanes // 2
            cos_half = jnp.broadcast_to(cos[:, middle : middle + 1], cos.shape)
            sin_half = jnp.broadcast_to(sin[:, middle : middle + 1], sin.shape)
            cos_step = cos_half * cos_half - sin_half * sin_half
            sin_step = 2.0 * (cos_half * sin_half)
            for lo in range(0, lons, lanes):
                if lo:
                    cos, sin = (
                        cos * cos_step - sin * sin_step,
                        sin * cos_step + cos * sin_step,
                    )
                part = scale[:, lo : lo + lanes]
                out_ref[0, pl.ds(at, tile), lo : lo + lanes] = (cos * part).astype(
                    jnp.bfloat16
                )
                out_ref[0, pl.ds(half + at, tile), lo : lo + lanes] = (-sin * part).astype(
                    jnp.bfloat16
                )
            return carry

        lax.fori_loop(0, half // tile, rows, 0)
        first += half


def dft_weights(points, chunks, lon_count):
    lats = points.shape[0]
    shapes = [(lats, 2 * waves.size, lon_count) for waves in chunks]
    wave = jnp.concatenate([waves.reshape(-1) for waves in chunks])
    wave = 4.0 * wave.astype(jnp.float32)[:, None]
    return pl.pallas_call(
        weights_kernel,
        grid_spec=pltpu.PrefetchScalarGridSpec(
            num_scalar_prefetch=1,
            grid=(lats,),
            in_specs=[pl.BlockSpec(wave.shape, lambda i, p: (0, 0))],
            out_specs=[pl.BlockSpec((1,) + sh[1:], lambda i, p: (i, 0, 0)) for sh in shapes],
        ),
        out_shape=[jax.ShapeDtypeStruct(sh, jnp.bfloat16) for sh in shapes],
        cost_estimate=pl.CostEstimate(
            flops=20 * lats * wave.shape[0] * lon_count,
            bytes_accessed=4 * lats * wave.shape[0] * lon_count,
            transcendentals=0,
        ),
        name="weights",
    )(points, wave)


def dft_kernel(weight_ref, grid_ref, out_ref):
    lons = grid_ref.shape[0] * grid_ref.shape[2]
    owners, _, parts, slots, levels = out_ref.shape
    half = owners * slots
    for i in range(grid_ref.shape[1]):
        column = grid_ref[:, i].reshape(lons, levels)
        result = jnp.dot(weight_ref[i], column, preferred_element_type=jnp.float32)
        for p in range(parts):
            piece = result[p * half : (p + 1) * half].reshape(owners, slots, levels)
            out_ref[:, i, p] = piece.astype(jnp.bfloat16)


def dft(weights, grid_field, owners):
    lats, cols, lons = weights.shape
    ranks, _, lon_local, levels = grid_field.shape
    slots = cols // (2 * owners)
    block = max(d for d in range(1, 9) if lats % d == 0)
    return pl.pallas_call(
        dft_kernel,
        grid=(lats // block,),
        in_specs=[
            pl.BlockSpec((block, cols, lons), lambda i: (i, 0, 0)),
            pl.BlockSpec((ranks, block, lon_local, levels), lambda i: (0, i, 0, 0)),
        ],
        out_specs=pl.BlockSpec((owners, block, 2, slots, levels), lambda i: (0, i, 0, 0, 0)),
        out_shape=jax.ShapeDtypeStruct((owners, lats, 2, slots, levels), jnp.bfloat16),
        cost_estimate=pl.CostEstimate(
            flops=2 * lats * cols * lons * levels,
            bytes_accessed=2 * lats * (cols * lons + (cols + lons) * levels),
            transcendentals=0,
        ),
        name="dft",
    )(weights, grid_field)


def per_device_plain(
    control, vertical_root, legendre, band_filter, row_plan, wave_order, lat_points, support
):
    owners = lax.axis_size("col")
    band_id = row_plan[0, 0]
    level_start = row_plan[0, 1]
    root_band = lax.dynamic_index_in_dim(vertical_root, band_id, 0, keepdims=False)
    level = jnp.arange(root_band.shape[1], dtype=jnp.int32)
    inside = (level >= level_start) & (level < level_start + LVR)
    root_block = jnp.where(inside[None, :], root_band, jnp.zeros_like(root_band))
    columns = control[0]
    lon_local, lat_count, _ = columns.shape
    rooted = jnp.einsum(
        "jik,kl->ijl", columns, root_block, preferred_element_type=jnp.float32
    ).astype(jnp.bfloat16)
    rooted = rooted.reshape(owners, lat_count // owners, lon_local, -1)
    grid_field = lax.all_to_all(rooted, "col", split_axis=0, concat_axis=0, tiled=True)
    lon_count = lon_local * owners
    lat_local = lat_count // owners

    slot_count = legendre.shape[0]
    degree_count = legendre.shape[2]
    ends = [slot_count * sum(CHUNKS[: c + 1]) // sum(CHUNKS) for c in range(len(CHUNKS))]
    spans = list(zip([0] + ends[:-1], ends))
    waves = wave_order.reshape(owners, slot_count)
    owned_waves = lax.dynamic_index_in_dim(waves, lax.axis_index("col"), 0, keepdims=False)
    degree = jnp.arange(degree_count, dtype=jnp.int32)
    bounds = lax.dynamic_index_in_dim(support, band_id, 0, keepdims=False)
    filter_row = lax.dynamic_index_in_dim(band_filter, band_id, 0, keepdims=False)
    window = filter_row * ((degree >= bounds[0]) & (degree < bounds[1])).astype(jnp.float32)

    weights = dft_weights(lat_points, [waves[:, lo:hi] for lo, hi in spans], lon_count)
    outputs = []
    fourier = dft(weights[0], grid_field, owners)
    for c, (lo, hi) in enumerate(spans):
        owned = lax.all_to_all(fourier, "col", split_axis=0, concat_axis=0, tiled=True)
        if c + 1 < len(spans):
            fourier = dft(weights[c + 1], grid_field, owners)
        if c:
            fourier, owned, _ = lax.optimization_barrier((fourier, owned, contribution))
        else:
            fourier, owned = lax.optimization_barrier((fourier, owned))
        owned = owned.reshape(lat_count, 2, hi - lo, owned.shape[4])
        spectral = jnp.einsum(
            "xpsl,sxn->snpl",
            owned,
            legendre[lo:hi],
            preferred_element_type=jnp.float32,
        )
        spectral_weight = (degree[None, :] >= owned_waves[lo:hi][:, None]).astype(
            jnp.float32
        ) * window[None, :]
        contribution = (spectral * spectral_weight[:, :, None, None]).astype(jnp.bfloat16)
        if c:
            contribution, outputs[-1] = lax.optimization_barrier((contribution, outputs[-1]))
        outputs.append(
            lax.psum_scatter(contribution, "band", scatter_dimension=1, tiled=True)
        )
    return jnp.concatenate(outputs, axis=0).astype(jnp.float32)


def greet(axes):
    barrier = pltpu.get_barrier_semaphore()
    total = 0
    for axis in axes:
        size, me = lax.axis_size(axis), lax.axis_index(axis)
        for d in range(1, size):
            pl.semaphore_signal(
                barrier,
                inc=1,
                device_id={axis: lax.rem(me + d, size)},
                device_id_type=MESH,
            )
        total += size - 1
    pl.semaphore_wait(barrier, total)


def lat_weights(count, wave_ref, lons, out_ref, index, tile):
    full = 4.0 * count
    inverse = 1.0 / full
    unit = (2.0 * math.pi) * inverse
    lon = lax.broadcasted_iota(jnp.int32, (1, lons), 1).astype(jnp.float32)
    scale = jnp.where(lon < count, lax.rsqrt(count), 0.0)
    nearest = 1.5 * 2.0**23
    half = wave_ref.shape[0]

    def rows(k, carry):
        at = pl.multiple_of(k * tile, tile)
        turns = wave_ref[pl.ds(at, tile), :] * lon[:, :LANES]
        whole = (turns * inverse + nearest) - nearest
        rest = turns - whole * full
        cos = sine((count - jnp.abs(rest)) * unit)
        away = jnp.abs(rest - count)
        sin = sine((jnp.minimum(away, full - away) - count) * unit)
        middle = LANES // 2
        cos_half = jnp.broadcast_to(cos[:, middle : middle + 1], cos.shape)
        sin_half = jnp.broadcast_to(sin[:, middle : middle + 1], sin.shape)
        cos_step = cos_half * cos_half - sin_half * sin_half
        sin_step = 2.0 * (cos_half * sin_half)
        for lo in range(0, lons, LANES):
            if lo:
                cos, sin = (
                    cos * cos_step - sin * sin_step,
                    sin * cos_step + cos * sin_step,
                )
            part = scale[:, lo : lo + LANES]
            out_ref[index, pl.ds(at, tile), lo : lo + LANES] = (cos * part).astype(
                jnp.bfloat16
            )
            out_ref[index, pl.ds(half + at, tile), lo : lo + LANES] = (
                sin * part
            ).astype(jnp.bfloat16)
        return carry

    lax.fori_loop(0, half // tile, rows, 0)


def chain_kernel(
    points_ref,
    plan_ref,
    order_ref,
    filter_ref,
    support_ref,
    rooted_ref,
    legendre_ref,
    out_ref,
    wave,
    window,
    block,
    wide,
    sent,
    got,
    weight,
    turned,
    fourier,
    owned,
    leg,
    leg_t,
    last,
    part,
    other,
    summed,
    block_sem,
    send_sem,
    recv_sem,
    own_sem,
    send2_sem,
    recv2_sem,
    own2_sem,
    leg_sem,
    part_sem,
    other_sem,
    out_sem,
):
    chunks, owners, _, lon_local, _ = sent.shape
    groups = fourier.shape[0]
    blocks = block.shape[0]
    bands, _, _, degrees, _ = part.shape[1:]
    lons = owners * lon_local
    lats = owners * chunks * 8
    waves, total = wave.shape[0], window.shape[0]
    eighth = waves // 8
    pairs = blocks // chunks
    early = chunks - 1
    cut = (PACK + 1) // 2
    pace = part_sem.shape[1]
    run = 8 // pace
    me, band = lax.axis_index("col"), lax.axis_index("band")

    lane = lax.broadcasted_iota(jnp.int32, (1, LANES), 1)
    rel = lane - plan_ref[0, 1]
    rel = jnp.where(rel < 0, rel + LANES, rel)
    spare = rel >= LVR

    def load_block(i):
        at = pl.multiple_of(16 * i, 16)
        return pltpu.make_async_copy(
            rooted_ref.at[:, pl.ds(at, 16), :], block.at[i], block_sem.at[i]
        )

    def across(src, dst, send, recv, to):
        return pltpu.make_async_remote_copy(
            src_ref=src,
            dst_ref=dst,
            send_sem=send,
            recv_sem=recv,
            device_id={"col": to},
            device_id_type=MESH,
        )

    def grid_copy(k, d):
        to = lax.rem(me + d, owners)
        return across(
            sent.at[k, to], got.at[k, me], send_sem.at[k, d], recv_sem.at[k, d], to
        )

    def grid_own(k):
        return pltpu.make_async_copy(sent.at[k, me], got.at[k, me], own_sem.at[k])

    def grid_send(k):
        for d in range(1, owners):
            grid_copy(k, d).start()
        grid_own(k).start()

    def view(ref, c, dev, piece):
        if piece == "early":
            return ref.at[c, dev, pl.ds(0, early)]
        if piece == "late":
            return ref.at[c, dev, pl.ds(early, 1)]
        if piece == "low":
            return ref.at[c, dev, :, pl.ds(0, cut)]
        if piece == "high":
            return ref.at[c, dev, :, pl.ds(cut, PACK - cut)]
        return ref.at[c, dev]

    def wave_copy(c, d, piece):
        to = lax.rem(me + d, owners)
        e = 1 if piece in ("late", "high") else 0
        return across(
            view(fourier, c, to, piece),
            view(owned, c, me, piece),
            send2_sem.at[c, d, e],
            recv2_sem.at[c, d, e],
            to,
        )

    def wave_own(c):
        return pltpu.make_async_copy(fourier.at[c, me], owned.at[c, me], own2_sem.at[c])

    def wave_start(c, piece):
        for d in range(1, owners):
            wave_copy(c, d, piece).start()

    def wave_wait(c, piece):
        for d in range(1, owners):
            wave_copy(c, d, piece).wait()

    def load_leg(c):
        at = pl.multiple_of(8 * c, 8)
        return pltpu.make_async_copy(
            legendre_ref.at[pl.ds(at, 8)], leg.at[lax.rem(c, 2)], leg_sem.at[c]
        )

    def give(c, h, d):
        to = lax.rem(band + d, bands)
        return pltpu.make_async_remote_copy(
            src_ref=part.at[lax.rem(c, 2), to, pl.ds(run * h, run)],
            dst_ref=other.at[d - 1, c, pl.ds(run * h, run)],
            send_sem=part_sem.at[c, h, d],
            recv_sem=other_sem.at[c, h, d],
            device_id={"band": to},
            device_id_type=MESH,
        )

    def out_copy(c):
        at = pl.multiple_of(8 * c, 8)
        return pltpu.make_async_copy(
            summed.at[lax.rem(c, 2)], out_ref.at[pl.ds(at, 8)], out_sem.at[c]
        )

    order = sorted(
        range(chunks), key=lambda o: (min((2 * o) % chunks, (2 * o + 1) % chunks), o)
    )
    for o in order:

        def load(b, carry, o=o):
            load_block(chunks * b + o).start()
            return carry

        lax.fori_loop(0, pairs, load, 0)
    for c in range(2):
        load_leg(c).start()
    greet(["col", "band"])

    filled = [0] * chunks
    begun = 0
    for o in order:

        def pack(b, carry, o=o):
            i = chunks * b + o
            load_block(i).wait()
            wide[...] = block[i].reshape(lon_local * 16, LANES).astype(jnp.float32)
            for h in range(2):
                q = 2 * o + h
                to, k = 2 * b + q // chunks, q % chunks
                extra = wide[pl.ds(8 * h + PACK, lon_local, stride=16), :]
                for g in range(PACK):
                    mine = wide[pl.ds(8 * h + g, lon_local, stride=16), :]
                    moved = pltpu.roll(extra, LVR - GROUP * g, 1)
                    sent[k, to, g] = jnp.where(spare, moved, mine).astype(jnp.bfloat16)
            return carry

        lax.fori_loop(0, pairs, pack, 0)
        for h in range(2):
            filled[(2 * o + h) % chunks] += 1
        while begun < 2 and filled[begun] == 2:
            grid_send(begun)
            begun += 1

    def wave_row(r, carry):
        sl, rest = r // eighth, lax.rem(r, eighth)
        c, dev = rest // owners, lax.rem(rest, owners)
        value = order_ref[dev * (8 * groups) + 8 * c + sl]
        wave[pl.ds(r, 1), :] = jnp.full((1, LANES), 4 * value, jnp.int32).astype(jnp.float32)
        return carry

    lax.fori_loop(0, waves, wave_row, 0)
    band_id = plan_ref[0, 0]
    lower, upper = support_ref[band_id, 0], support_ref[band_id, 1]

    def window_row(n, carry):
        row = jnp.full((1, LANES), filter_ref[band_id, n], jnp.float32)
        at = jnp.full((1, LANES), n, jnp.int32)
        live = (at >= lower) & (at < upper) & (rel < LVR)
        window[pl.ds(n, 1), :] = jnp.where(live, row, 0.0)
        return carry

    lax.fori_loop(0, total, window_row, 0)

    def transform(k, lat, x):
        for p in range(2):
            res = jnp.dot(
                weight[lat, p * waves : (p + 1) * waves, :],
                x,
                preferred_element_type=jnp.float32,
            )
            extra = res[PACK * eighth :]
            for g in range(PACK):
                moved = pltpu.roll(extra, LVR - GROUP * g, 1)
                piece = jnp.where(spare, moved, res[g * eighth : (g + 1) * eighth])
                turned[pl.ds(g * eighth * 16 + p * 8 + lat, eighth, stride=16), :] = piece

    def chunk(k, carry):
        def make(lat, c):
            count = jnp.full((1, 1), points_ref[8 * k + lat], jnp.int32).astype(jnp.float32)
            lat_weights(count, wave, lons, weight, lat, 32 if waves % 32 == 0 else 8)
            return c

        lax.fori_loop(0, 8, make, 0)
        for d in range(1, owners):
            grid_copy(k, d).wait()
        grid_own(k).wait()

        @pl.when(k + 2 < chunks)
        def _():
            grid_send(k + 2)

        def plain(g, c):
            transform(k, g, got[k, :, g].reshape(lons, LANES))
            return c

        lax.fori_loop(0, PACK, plain, 0)
        x = jnp.zeros((lons, LANES), jnp.float32)
        for g in range(PACK):
            moved = got[k, :, g].reshape(lons, LANES).astype(jnp.float32)
            moved = pltpu.roll(moved, LANES - LVR + GROUP * g, 1)
            x = jnp.where((rel >= GROUP * g) & (rel < GROUP * (g + 1)), moved, x)
        transform(k, PACK, x.astype(jnp.bfloat16))
        for c in range(groups):
            for g in range(PACK):
                at = (g * eighth + c * owners) * 16
                rows = turned[at : at + 16 * owners, :].reshape(owners, 16, LANES)
                fourier[c, :, k, g] = rows.astype(jnp.bfloat16)

        @pl.when(k == early - 1)
        def _():
            wave_start(0, "early")

        return carry

    lax.fori_loop(0, chunks, chunk, 0)
    wave_start(0, "late")
    wave_own(0).start()
    wave_start(1, "all")
    wave_own(1).start()

    def finish(c):
        for h in range(pace):
            for d in range(1, bands):
                give(c, h, d).wait_recv()
            for sl in range(run * h, run * (h + 1)):
                for p in range(2):
                    acc = part[lax.rem(c, 2), band, sl, p].astype(jnp.float32)
                    for d in range(1, bands):
                        acc = acc + other[d - 1, c, sl, p].astype(jnp.float32)
                    summed[lax.rem(c, 2), sl, pl.ds(p, degrees, stride=2), :] = acc

    def slot_out(c, sl, halves):
        res = jnp.dot(
            leg_t[sl],
            jnp.concatenate([h.astype(jnp.bfloat16) for h in halves], axis=1),
            preferred_element_type=jnp.float32,
        )
        degree = lax.broadcasted_iota(jnp.int32, (total, LANES), 0)
        order_here = order_ref[me * (8 * groups) + 8 * c + sl]
        keep = jnp.where(degree >= order_here, window[...], 0.0)
        for p in range(2):
            value = (res[:, p * LANES : (p + 1) * LANES] * keep).astype(jnp.bfloat16)
            part[lax.rem(c, 2), :, sl, p] = value.reshape(bands, degrees, LANES)
        if sl % run == run - 1:
            for d in range(1, bands):
                give(c, sl // run, d).start()

    def group(c, carry):
        load_leg(c).wait()
        for sl in range(8):
            leg_t[sl] = leg[lax.rem(c, 2), sl].T

        @pl.when(c + 2 < groups)
        def _():
            load_leg(c + 2).start()

        @pl.when(c == 0)
        def _():
            wave_wait(c, "early")
            wave_wait(c, "late")

        @pl.when((c > 0) & (c < groups - 1))
        def _():
            wave_wait(c, "all")

        @pl.when(c == groups - 1)
        def _():
            wave_wait(c, "low")

        wave_own(c).wait()

        @pl.when(c + 2 < groups - 1)
        def _():
            wave_start(c + 2, "all")
            wave_own(c + 2).start()

        @pl.when(c + 2 == groups - 1)
        def _():
            wave_start(c + 2, "low")
            wave_start(c + 2, "high")
            wave_own(c + 2).start()

        @pl.when(c >= 2)
        def _():
            for h in range(pace):
                for d in range(1, bands):
                    give(c - 2, h, d).wait_send()

        for sl in range(PACK):
            if sl == cut:

                @pl.when(c == groups - 1)
                def _():
                    wave_wait(c, "high")

            value = owned[c, :, :, sl].astype(jnp.float32).reshape(lats // 8, 2, 8, LANES)
            halves = [value[:, p].reshape(lats, LANES) for p in range(2)]
            here = (rel >= GROUP * sl) & (rel < GROUP * (sl + 1))
            for p in range(2):
                moved = pltpu.roll(halves[p], LANES - LVR + GROUP * sl, 1)
                before = last[p] if sl else jnp.zeros((lats, LANES), jnp.float32)
                last[p] = jnp.where(here, moved, before)
            slot_out(c, sl, halves)
        slot_out(c, PACK, [last[0], last[1]])

        @pl.when(c >= 3)
        def _():
            out_copy(c - 3).wait()

        @pl.when(c >= 1)
        def _():
            finish(c - 1)
            out_copy(c - 1).start()

        return carry

    lax.fori_loop(0, groups, group, 0)
    out_copy(groups - 3).wait()
    finish(groups - 1)
    out_copy(groups - 1).start()
    for c in range(groups - 2, groups):
        for h in range(pace):
            for d in range(1, bands):
                give(c, h, d).wait_send()
        out_copy(c).wait()


def chain(points, plan, order, band_filter, support, rooted, legendre, owners, bands):
    lon_local, lats, _ = rooted.shape
    slot_count, _, total = legendre.shape
    waves = order.shape[0]
    chunks, groups, blocks = lats // owners // 8, slot_count // 8, lats // 16
    lons, degrees, pace = owners * lon_local, total // bands, 4
    bf16, f32 = jnp.bfloat16, jnp.float32
    any_spec = pl.BlockSpec(memory_space=pl.ANY)
    smem_spec = pl.BlockSpec(memory_space=pltpu.SMEM)
    dma = pltpu.SemaphoreType.DMA
    return pl.pallas_call(
        chain_kernel,
        in_specs=[smem_spec] * 5 + [any_spec] * 2,
        out_specs=any_spec,
        out_shape=jax.ShapeDtypeStruct((slot_count, 2 * degrees, LANES), f32),
        scratch_shapes=[
            pltpu.VMEM((waves, LANES), f32),
            pltpu.VMEM((total, LANES), f32),
            pltpu.VMEM((blocks, lon_local, 16, LANES), bf16),
            pltpu.VMEM((lon_local * 16, LANES), f32),
            pltpu.VMEM((chunks, owners, PACK, lon_local, LANES), bf16),
            pltpu.VMEM((chunks, owners, PACK, lon_local, LANES), bf16),
            pltpu.VMEM((8, 2 * waves, lons), bf16),
            pltpu.VMEM((PACK * waves // 8 * 16, LANES), f32),
            pltpu.VMEM((groups, owners, chunks, PACK, 16, LANES), bf16),
            pltpu.VMEM((groups, owners, chunks, PACK, 16, LANES), bf16),
            pltpu.VMEM((2, 8, lats, total), bf16),
            pltpu.VMEM((8, total, lats), bf16),
            pltpu.VMEM((2, lats, LANES), f32),
            pltpu.VMEM((2, bands, 8, 2, degrees, LANES), bf16),
            pltpu.VMEM((bands - 1, groups, 8, 2, degrees, LANES), bf16),
            pltpu.VMEM((2, 8, 2 * degrees, LANES), f32),
            dma((blocks,)),
            dma((chunks, owners)),
            dma((chunks, owners)),
            dma((chunks,)),
            dma((groups, owners, 2)),
            dma((groups, owners, 2)),
            dma((groups,)),
            dma((groups,)),
            dma((groups, pace, bands)),
            dma((groups, pace, bands)),
            dma((groups,)),
        ],
        compiler_params=pltpu.CompilerParams(
            collective_id=0, has_side_effects=True, vmem_limit_bytes=60 * 2**20
        ),
        name="chain",
    )(points, plan, order, band_filter, support, rooted, legendre)


def per_device_fused(
    control, vertical_root, legendre, band_filter, row_plan, wave_order, lat_points, support
):
    root = lax.dynamic_index_in_dim(vertical_root, row_plan[0, 0], 0, keepdims=False)
    rooted = jnp.einsum(
        "jik,kl->jil", control[0], root, preferred_element_type=jnp.float32
    ).astype(jnp.bfloat16)
    bands = lax.axis_size("band")
    result = chain(
        lat_points,
        row_plan,
        wave_order,
        band_filter,
        support,
        rooted,
        legendre,
        lax.axis_size("col"),
        bands,
    )
    slot_count, _, total = legendre.shape
    return result.reshape(slot_count, total // bands, 2, LANES)


def per_device(control, vertical_root, legendre, *rest):
    owners, bands = lax.axis_size("col"), lax.axis_size("band")
    _, lon_local, lats, _ = control.shape
    slot_count, _, total = legendre.shape
    chunks = lats // owners // 8
    fits = (
        vertical_root.shape[2] == LANES
        and lats % (16 * owners // math.gcd(owners, 2)) == 0
        and lats % (8 * owners) == 0
        and owners % 2 == 0
        and chunks % 2 == 1
        and lon_local % 16 == 0
        and (owners * lon_local) % LANES == 0
        and chunks >= 3
        and slot_count % 8 == 0
        and slot_count >= 24
        and (slot_count // 8 * owners) % 8 == 0
        and total % bands == 0
        and (total // bands) % 16 == 0
        and bands > 1
    )
    body = per_device_fused if fits else per_device_plain
    return body(control, vertical_root, legendre, *rest)


def solution(mesh):
    in_specs = (
        P("band", "col", None, None),
        P(),
        P("col", None, None),
        P(),
        P("band", None),
        P(),
        P("col"),
        P(),
    )
    out_specs = P("col", "band", None, None)
    return jax.shard_map(
        per_device, mesh=mesh, in_specs=in_specs, out_specs=out_specs, check_vma=False
    )
```

```python
import functools
import math

import jax
import jax.numpy as jnp
from jax import lax
from jax.experimental import pallas as pl
from jax.experimental.pallas import tpu as pltpu
from jax.sharding import PartitionSpec as P

LVR = 112
CHUNKS = (2, 2, 1)
LANES = 128
GROUP = 16
DEPTH = 2
VMEM_LIMIT = 51 * 2**20
PACK = LVR // GROUP
MESH = pl.DeviceIdType.MESH


def sine(theta):
    square = theta * theta
    value = -1.0 / 39916800.0 * square + 1.0 / 362880.0
    value = value * square - 1.0 / 5040.0
    value = value * square + 1.0 / 120.0
    value = value * square - 1.0 / 6.0
    value = value * square + 1.0
    return value * theta


def weights_kernel(points_ref, wave_ref, *out_refs):
    count = jnp.full((1, 1), points_ref[pl.program_id(0)], jnp.int32).astype(jnp.float32)
    lons = out_refs[0].shape[2]
    lanes = 128
    lon = lax.broadcasted_iota(jnp.int32, (1, lons), 1).astype(jnp.float32)
    full = 4.0 * count
    inverse = 1.0 / full
    unit = (2.0 * math.pi) * inverse
    scale = jnp.where(lon < count, lax.rsqrt(count), 0.0)
    nearest = 1.5 * 2.0**23
    first = 0
    for out_ref in out_refs:
        half = out_ref.shape[1] // 2
        tile = 8 if half % 16 else 16

        def rows(k, carry, out_ref=out_ref, first=first, tile=tile, half=half):
            at = pl.multiple_of(k * tile, tile)
            turns = wave_ref[pl.ds(first + at, tile), :] * lon[:, :lanes]
            whole = (turns * inverse + nearest) - nearest
            rest = turns - whole * full
            cos = sine((count - jnp.abs(rest)) * unit)
            away = jnp.abs(rest - count)
            sin = sine((count - jnp.minimum(away, full - away)) * unit)
            middle = lanes // 2
            cos_half = jnp.broadcast_to(cos[:, middle : middle + 1], cos.shape)
            sin_half = jnp.broadcast_to(sin[:, middle : middle + 1], sin.shape)
            cos_step = cos_half * cos_half - sin_half * sin_half
            sin_step = 2.0 * (cos_half * sin_half)
            for lo in range(0, lons, lanes):
                if lo:
                    cos, sin = (
                        cos * cos_step - sin * sin_step,
                        sin * cos_step + cos * sin_step,
                    )
                part = scale[:, lo : lo + lanes]
                out_ref[0, pl.ds(at, tile), lo : lo + lanes] = (cos * part).astype(
                    jnp.bfloat16
                )
                out_ref[0, pl.ds(half + at, tile), lo : lo + lanes] = (-sin * part).astype(
                    jnp.bfloat16
                )
            return carry

        lax.fori_loop(0, half // tile, rows, 0)
        first += half


def dft_weights(points, chunks, lon_count):
    lats = points.shape[0]
    shapes = [(lats, 2 * waves.size, lon_count) for waves in chunks]
    wave = jnp.concatenate([waves.reshape(-1) for waves in chunks])
    wave = 4.0 * wave.astype(jnp.float32)[:, None]
    return pl.pallas_call(
        weights_kernel,
        grid_spec=pltpu.PrefetchScalarGridSpec(
            num_scalar_prefetch=1,
            grid=(lats,),
            in_specs=[pl.BlockSpec(wave.shape, lambda i, p: (0, 0))],
            out_specs=[pl.BlockSpec((1,) + sh[1:], lambda i, p: (i, 0, 0)) for sh in shapes],
        ),
        out_shape=[jax.ShapeDtypeStruct(sh, jnp.bfloat16) for sh in shapes],
        cost_estimate=pl.CostEstimate(
            flops=20 * lats * wave.shape[0] * lon_count,
            bytes_accessed=4 * lats * wave.shape[0] * lon_count,
            transcendentals=0,
        ),
        name="weights",
    )(points, wave)


def dft_kernel(weight_ref, grid_ref, out_ref):
    lons = grid_ref.shape[0] * grid_ref.shape[2]
    owners, _, parts, slots, levels = out_ref.shape
    half = owners * slots
    for i in range(grid_ref.shape[1]):
        column = grid_ref[:, i].reshape(lons, levels)
        result = jnp.dot(weight_ref[i], column, preferred_element_type=jnp.float32)
        for p in range(parts):
            piece = result[p * half : (p + 1) * half].reshape(owners, slots, levels)
            out_ref[:, i, p] = piece.astype(jnp.bfloat16)


def dft(weights, grid_field, owners):
    lats, cols, lons = weights.shape
    ranks, _, lon_local, levels = grid_field.shape
    slots = cols // (2 * owners)
    block = max(d for d in range(1, 9) if lats % d == 0)
    return pl.pallas_call(
        dft_kernel,
        grid=(lats // block,),
        in_specs=[
            pl.BlockSpec((block, cols, lons), lambda i: (i, 0, 0)),
            pl.BlockSpec((ranks, block, lon_local, levels), lambda i: (0, i, 0, 0)),
        ],
        out_specs=pl.BlockSpec((owners, block, 2, slots, levels), lambda i: (0, i, 0, 0, 0)),
        out_shape=jax.ShapeDtypeStruct((owners, lats, 2, slots, levels), jnp.bfloat16),
        cost_estimate=pl.CostEstimate(
            flops=2 * lats * cols * lons * levels,
            bytes_accessed=2 * lats * (cols * lons + (cols + lons) * levels),
            transcendentals=0,
        ),
        name="dft",
    )(weights, grid_field)


def per_device_plain(
    control, vertical_root, legendre, band_filter, row_plan, wave_order, lat_points, support
):
    owners = lax.axis_size("col")
    band_id = row_plan[0, 0]
    level_start = row_plan[0, 1]
    root_band = lax.dynamic_index_in_dim(vertical_root, band_id, 0, keepdims=False)
    level = jnp.arange(root_band.shape[1], dtype=jnp.int32)
    inside = (level >= level_start) & (level < level_start + LVR)
    root_block = jnp.where(inside[None, :], root_band, jnp.zeros_like(root_band))
    columns = control[0]
    lon_local, lat_count, _ = columns.shape
    rooted = jnp.einsum(
        "jik,kl->ijl", columns, root_block, preferred_element_type=jnp.float32
    ).astype(jnp.bfloat16)
    rooted = rooted.reshape(owners, lat_count // owners, lon_local, -1)
    grid_field = lax.all_to_all(rooted, "col", split_axis=0, concat_axis=0, tiled=True)
    lon_count = lon_local * owners
    lat_local = lat_count // owners

    slot_count = legendre.shape[0]
    degree_count = legendre.shape[2]
    ends = [slot_count * sum(CHUNKS[: c + 1]) // sum(CHUNKS) for c in range(len(CHUNKS))]
    spans = list(zip([0] + ends[:-1], ends))
    waves = wave_order.reshape(owners, slot_count)
    owned_waves = lax.dynamic_index_in_dim(waves, lax.axis_index("col"), 0, keepdims=False)
    degree = jnp.arange(degree_count, dtype=jnp.int32)
    bounds = lax.dynamic_index_in_dim(support, band_id, 0, keepdims=False)
    filter_row = lax.dynamic_index_in_dim(band_filter, band_id, 0, keepdims=False)
    window = filter_row * ((degree >= bounds[0]) & (degree < bounds[1])).astype(jnp.float32)

    weights = dft_weights(lat_points, [waves[:, lo:hi] for lo, hi in spans], lon_count)
    outputs = []
    fourier = dft(weights[0], grid_field, owners)
    for c, (lo, hi) in enumerate(spans):
        owned = lax.all_to_all(fourier, "col", split_axis=0, concat_axis=0, tiled=True)
        if c + 1 < len(spans):
            fourier = dft(weights[c + 1], grid_field, owners)
        if c:
            fourier, owned, _ = lax.optimization_barrier((fourier, owned, contribution))
        else:
            fourier, owned = lax.optimization_barrier((fourier, owned))
        owned = owned.reshape(lat_count, 2, hi - lo, owned.shape[4])
        spectral = jnp.einsum(
            "xpsl,sxn->snpl",
            owned,
            legendre[lo:hi],
            preferred_element_type=jnp.float32,
        )
        spectral_weight = (degree[None, :] >= owned_waves[lo:hi][:, None]).astype(
            jnp.float32
        ) * window[None, :]
        contribution = (spectral * spectral_weight[:, :, None, None]).astype(jnp.bfloat16)
        if c:
            contribution, outputs[-1] = lax.optimization_barrier((contribution, outputs[-1]))
        outputs.append(
            lax.psum_scatter(contribution, "band", scatter_dimension=1, tiled=True)
        )
    return jnp.concatenate(outputs, axis=0).astype(jnp.float32)


def greet(axes):
    barrier = pltpu.get_barrier_semaphore()
    total = 0
    for axis in axes:
        size, me = lax.axis_size(axis), lax.axis_index(axis)
        for d in range(1, size):
            pl.semaphore_signal(
                barrier,
                inc=1,
                device_id={axis: lax.rem(me + d, size)},
                device_id_type=MESH,
            )
        total += size - 1
    pl.semaphore_wait(barrier, total)


def lat_weights(count, wave_ref, lons, out_ref, index, tile):
    full = 4.0 * count
    inverse = 1.0 / full
    unit = (2.0 * math.pi) * inverse
    lon = lax.broadcasted_iota(jnp.int32, (1, lons), 1).astype(jnp.float32)
    scale = jnp.where(lon < count, lax.rsqrt(count), 0.0)
    nearest = 1.5 * 2.0**23
    half = wave_ref.shape[0]

    def rows(k, carry):
        at = pl.multiple_of(k * tile, tile)
        turns = wave_ref[pl.ds(at, tile), :] * lon[:, :LANES]
        whole = (turns * inverse + nearest) - nearest
        rest = turns - whole * full
        cos = sine((count - jnp.abs(rest)) * unit)
        away = jnp.abs(rest - count)
        sin = sine((jnp.minimum(away, full - away) - count) * unit)
        middle = LANES // 2
        cos_half = jnp.broadcast_to(cos[:, middle : middle + 1], cos.shape)
        sin_half = jnp.broadcast_to(sin[:, middle : middle + 1], sin.shape)
        cos_step = cos_half * cos_half - sin_half * sin_half
        sin_step = 2.0 * (cos_half * sin_half)
        for lo in range(0, lons, LANES):
            if lo:
                cos, sin = (
                    cos * cos_step - sin * sin_step,
                    sin * cos_step + cos * sin_step,
                )
            part = scale[:, lo : lo + LANES]
            out_ref[index, pl.ds(at, tile), lo : lo + LANES] = (cos * part).astype(
                jnp.bfloat16
            )
            out_ref[index, pl.ds(half + at, tile), lo : lo + LANES] = (
                sin * part
            ).astype(jnp.bfloat16)
        return carry

    lax.fori_loop(0, half // tile, rows, 0)


def pack_plan(chunks):
    steps = sorted(
        ((o, h) for o in range(chunks) for h in range(2)),
        key=lambda s: ((2 * s[0] + s[1]) % chunks, s),
    )
    slot_of, freed, seen, ready = {}, {}, {}, {}
    slots = 0
    for i, (o, h) in enumerate(steps):
        if o not in slot_of:
            free = [s for s, t in freed.items() if t <= i - 2]
            if free:
                slot_of[o] = free[0]
                ready[o] = freed.pop(free[0])
            else:
                slot_of[o], ready[o] = slots, -1
                slots += 1
        seen[o] = seen.get(o, 0) + 1
        if seen[o] == 2:
            freed[slot_of[o]] = i
    return steps, slot_of, ready, slots


def chain_kernel(
    points_ref,
    plan_ref,
    order_ref,
    filter_ref,
    support_ref,
    rooted_ref,
    legendre_ref,
    out_ref,
    wave,
    window,
    block,
    wide,
    sent,
    got,
    weight,
    turned,
    fourier,
    owned,
    leg,
    leg_t,
    last,
    part,
    other,
    summed,
    block_sem,
    send_sem,
    recv_sem,
    own_sem,
    send2_sem,
    recv2_sem,
    own2_sem,
    leg_sem,
    part_sem,
    other_sem,
    out_sem,
):
    chunks, owners, _, lon_local, _ = sent.shape
    groups = fourier.shape[0]
    pairs = block.shape[1]
    bands, _, _, degrees, _ = part.shape[1:]
    lons = owners * lon_local
    lats = owners * chunks * 8
    waves, total = wave.shape[0], window.shape[0]
    eighth = waves // 8
    early = chunks - 1
    pace = part_sem.shape[1]
    run = 8 // pace
    me, band = lax.axis_index("col"), lax.axis_index("band")

    lane = lax.broadcasted_iota(jnp.int32, (1, LANES), 1)
    rel = lane - plan_ref[0, 1]
    rel = jnp.where(rel < 0, rel + LANES, rel)
    spare = rel >= LVR

    steps, slot_of, ready, _ = pack_plan(chunks)

    def load_block(o, b):
        at = pl.multiple_of(16 * (chunks * b + o), 16)
        return pltpu.make_async_copy(
            rooted_ref.at[:, pl.ds(at, 16), :], block.at[slot_of[o], b], block_sem.at[o, b]
        )

    def load_blocks(o):
        for b in range(pairs):
            load_block(o, b).start()

    def across(src, dst, send, recv, to):
        return pltpu.make_async_remote_copy(
            src_ref=src,
            dst_ref=dst,
            send_sem=send,
            recv_sem=recv,
            device_id={"col": to},
            device_id_type=MESH,
        )

    def grid_copy(k, d):
        to = lax.rem(me + d, owners)
        return across(
            sent.at[k, to], got.at[k, me], send_sem.at[k, d], recv_sem.at[k, d], to
        )

    def grid_own(k):
        return pltpu.make_async_copy(sent.at[k, me], got.at[k, me], own_sem.at[k])

    def grid_send(k):
        for d in range(1, owners):
            grid_copy(k, d).start()
        grid_own(k).start()

    def view(ref, c, dev, piece):
        if piece == "late":
            return ref.at[c, dev, pl.ds(early, 1)]
        first = piece % pace * run
        tiles = pl.ds(first, min(run, PACK - first))
        if piece >= pace:
            return ref.at[c, dev, pl.ds(0, early), tiles]
        return ref.at[c, dev, :, tiles]

    def wave_copy(c, d, piece):
        to = lax.rem(me + d, owners)
        e = pace if piece == "late" else piece % pace
        return across(
            view(fourier, c, to, piece),
            view(owned, c, me, piece),
            send2_sem.at[c, d, e],
            recv2_sem.at[c, d, e],
            to,
        )

    def wave_own(c):
        return pltpu.make_async_copy(fourier.at[c, me], owned.at[c, me], own2_sem.at[c])

    def wave_start(c, piece):
        for d in range(1, owners):
            wave_copy(c, d, piece).start()

    def wave_wait(c, piece):
        for d in range(1, owners):
            wave_copy(c, d, piece).wait()

    def load_leg(c):
        at = pl.multiple_of(8 * c, 8)
        return pltpu.make_async_copy(
            legendre_ref.at[pl.ds(at, 8)], leg.at[lax.rem(c, 2)], leg_sem.at[c]
        )

    def give(c, h, d):
        to = lax.rem(band + d, bands)
        return pltpu.make_async_remote_copy(
            src_ref=part.at[lax.rem(c, 2), to, pl.ds(run * h, run)],
            dst_ref=other.at[d - 1, c, pl.ds(run * h, run)],
            send_sem=part_sem.at[c, h, d],
            recv_sem=other_sem.at[c, h, d],
            device_id={"band": to},
            device_id_type=MESH,
        )

    def out_copy(c, h):
        at = pl.multiple_of(8 * c + run * h, run)
        return pltpu.make_async_copy(
            summed.at[lax.rem(c, 2), pl.ds(run * h, run)],
            out_ref.at[pl.ds(at, run)],
            out_sem.at[c, h],
        )

    for o in slot_of:
        if ready[o] < 0:
            load_blocks(o)
    for c in range(2):
        load_leg(c).start()
    greet(["col", "band"])

    def pack(o, h, first):
        q = 2 * o + h
        k = q % chunks

        def one(b, carry):
            if first:
                load_block(o, b).wait()
            wide[...] = block[slot_of[o], b].reshape(lon_local * 16, LANES).astype(jnp.float32)
            to = 2 * b + q // chunks
            extra = wide[pl.ds(8 * h + PACK, lon_local, stride=16), :]
            for g in range(PACK):
                mine = wide[pl.ds(8 * h + g, lon_local, stride=16), :]
                moved = pltpu.roll(extra, LVR - GROUP * g, 1)
                sent[k, to, g] = jnp.where(spare, moved, mine).astype(jnp.bfloat16)
            return carry

        lax.fori_loop(0, pairs, one, 0)

    for i, (o, h) in enumerate(steps):
        pack(o, h, o not in [s[0] for s in steps[:i]])
        for later in slot_of:
            if ready[later] == i:
                load_blocks(later)
        if i % 2 and i // 2 < 2:
            grid_send(i // 2)

    def wave_row(r, carry):
        sl, rest = r // eighth, lax.rem(r, eighth)
        c, dev = rest // owners, lax.rem(rest, owners)
        value = order_ref[dev * (8 * groups) + 8 * c + sl]
        wave[pl.ds(r, 1), :] = jnp.full((1, LANES), 4 * value, jnp.int32).astype(jnp.float32)
        return carry

    lax.fori_loop(0, waves, wave_row, 0)
    band_id = plan_ref[0, 0]
    lower, upper = support_ref[0, band_id], support_ref[1, band_id]

    def window_row(n, carry):
        row = jnp.full((1, LANES), filter_ref[band_id, n], jnp.float32)
        at = jnp.full((1, LANES), n, jnp.int32)
        live = (at >= lower) & (at < upper) & (rel < LVR)
        window[pl.ds(n, 1), :] = jnp.where(live, row, 0.0)
        return carry

    lax.fori_loop(0, total, window_row, 0)

    def transform(k, lat, x):
        for p in range(2):
            res = jnp.dot(
                weight[lat, p * waves : (p + 1) * waves, :],
                x,
                preferred_element_type=jnp.float32,
            )
            extra = res[PACK * eighth :]
            for g in range(PACK):
                moved = pltpu.roll(extra, LVR - GROUP * g, 1)
                piece = jnp.where(spare, moved, res[g * eighth : (g + 1) * eighth])
                turned[pl.ds(g * eighth * 16 + p * 8 + lat, eighth, stride=16), :] = piece

    def chunk(k, carry):
        def make(lat, c):
            count = jnp.full((1, 1), points_ref[8 * k + lat], jnp.int32).astype(jnp.float32)
            lat_weights(count, wave, lons, weight, lat, 32 if waves % 32 == 0 else 8)
            return c

        lax.fori_loop(0, 8, make, 0)
        for d in range(1, owners):
            grid_copy(k, d).wait()
        grid_own(k).wait()

        @pl.when(k + 2 < chunks)
        def _():
            grid_send(k + 2)

        @pl.when(k == chunks - 1)
        def _():
            for q in range(1, pace):
                wave_start(0, pace + q)

        def plain(g, c):
            transform(k, g, got[k, :, g].reshape(lons, LANES))
            return c

        lax.fori_loop(0, PACK, plain, 0)
        x = jnp.zeros((lons, LANES), jnp.float32)
        for g in range(PACK):
            moved = got[k, :, g].reshape(lons, LANES).astype(jnp.float32)
            moved = pltpu.roll(moved, LANES - LVR + GROUP * g, 1)
            x = jnp.where((rel >= GROUP * g) & (rel < GROUP * (g + 1)), moved, x)
        transform(k, PACK, x.astype(jnp.bfloat16))
        for c in range(groups):
            for g in range(PACK):
                at = (g * eighth + c * owners) * 16
                rows = turned[at : at + 16 * owners, :].reshape(owners, 16, LANES)
                fourier[c, :, k, g] = rows.astype(jnp.bfloat16)

        @pl.when(k == early - 1)
        def _():
            wave_start(0, pace)

        return carry

    lax.fori_loop(0, chunks, chunk, 0)
    wave_start(0, "late")
    wave_own(0).start()
    for q in range(DEPTH):
        wave_start(1, q)
    wave_own(1).start()

    def finish(c):
        for h in range(pace):
            for d in range(1, bands):
                give(c, h, d).wait_recv()
            for sl in range(run * h, run * (h + 1)):
                for p in range(2):
                    acc = part[lax.rem(c, 2), band, sl, p].astype(jnp.float32)
                    for d in range(1, bands):
                        acc = acc + other[d - 1, c, sl, p].astype(jnp.float32)
                    summed[lax.rem(c, 2), sl, pl.ds(p, degrees, stride=2), :] = acc
            out_copy(c, h).start()

    def slot_out(c, sl, halves):
        res = jnp.dot(
            leg_t[sl],
            jnp.concatenate([h.astype(jnp.bfloat16) for h in halves], axis=1),
            preferred_element_type=jnp.float32,
        )
        degree = lax.broadcasted_iota(jnp.int32, (total, LANES), 0)
        order_here = order_ref[me * (8 * groups) + 8 * c + sl]
        keep = jnp.where(degree >= order_here, window[...], 0.0)
        for p in range(2):
            value = (res[:, p * LANES : (p + 1) * LANES] * keep).astype(jnp.bfloat16)
            part[lax.rem(c, 2), :, sl, p] = value.reshape(bands, degrees, LANES)
        if sl % run == run - 1:
            for d in range(1, bands):
                give(c, sl // run, d).start()

    def group(c, carry):
        load_leg(c).wait()
        for sl in range(8):
            leg_t[sl] = leg[lax.rem(c, 2), sl].T

        @pl.when(c + 2 < groups)
        def _():
            load_leg(c + 2).start()

        def arrive(q):
            @pl.when(c == 0)
            def _():
                wave_wait(0, pace + q)
                if q == 0:
                    wave_wait(0, "late")

            @pl.when(c > 0)
            def _():
                wave_wait(c, q)
                if q + DEPTH < pace:
                    wave_start(c, q + DEPTH)

            @pl.when((c > 0) & (c + 1 < groups))
            def _():
                if q + DEPTH >= pace:
                    wave_start(c + 1, q + DEPTH - pace)

        arrive(0)
        wave_own(c).wait()

        @pl.when(c + 2 < groups)
        def _():
            wave_own(c + 2).start()

        @pl.when(c >= 2)
        def _():
            for h in range(pace):
                for d in range(1, bands):
                    give(c - 2, h, d).wait_send()

        for sl in range(PACK):
            if sl and sl % run == 0:
                arrive(sl // run)
            value = owned[c, :, :, sl].astype(jnp.float32).reshape(lats // 8, 2, 8, LANES)
            halves = [value[:, p].reshape(lats, LANES) for p in range(2)]
            here = (rel >= GROUP * sl) & (rel < GROUP * (sl + 1))
            for p in range(2):
                moved = pltpu.roll(halves[p], LANES - LVR + GROUP * sl, 1)
                before = last[p] if sl else jnp.zeros((lats, LANES), jnp.float32)
                last[p] = jnp.where(here, moved, before)
            slot_out(c, sl, halves)
        slot_out(c, PACK, [last[0], last[1]])

        @pl.when(c >= 3)
        def _():
            for h in range(pace):
                out_copy(c - 3, h).wait()

        @pl.when(c >= 1)
        def _():
            finish(c - 1)

        return carry

    lax.fori_loop(0, groups, group, 0)
    for h in range(pace):
        out_copy(groups - 3, h).wait()
    finish(groups - 1)
    for c in range(groups - 2, groups):
        for h in range(pace):
            for d in range(1, bands):
                give(c, h, d).wait_send()
            out_copy(c, h).wait()


def chain(points, plan, order, band_filter, support, rooted, legendre, owners, bands):
    lon_local, lats, _ = rooted.shape
    slot_count, _, total = legendre.shape
    waves = order.shape[0]
    chunks, groups = lats // owners // 8, slot_count // 8
    block_slots, pairs = pack_plan(chunks)[3], lats // 16 // chunks
    lons, degrees, pace = owners * lon_local, total // bands, 4
    bf16, f32 = jnp.bfloat16, jnp.float32
    any_spec = pl.BlockSpec(memory_space=pl.ANY)
    smem_spec = pl.BlockSpec(memory_space=pltpu.SMEM)
    dma = pltpu.SemaphoreType.DMA
    return pl.pallas_call(
        chain_kernel,
        in_specs=[smem_spec] * 5 + [any_spec] * 2,
        out_specs=any_spec,
        out_shape=jax.ShapeDtypeStruct((slot_count, 2 * degrees, LANES), f32),
        scratch_shapes=[
            pltpu.VMEM((waves, LANES), f32),
            pltpu.VMEM((total, LANES), f32),
            pltpu.VMEM((block_slots, pairs, lon_local, 16, LANES), bf16),
            pltpu.VMEM((lon_local * 16, LANES), f32),
            pltpu.VMEM((chunks, owners, PACK, lon_local, LANES), bf16),
            pltpu.VMEM((chunks, owners, PACK, lon_local, LANES), bf16),
            pltpu.VMEM((8, 2 * waves, lons), bf16),
            pltpu.VMEM((PACK * waves // 8 * 16, LANES), f32),
            pltpu.VMEM((groups, owners, chunks, PACK, 16, LANES), bf16),
            pltpu.VMEM((groups, owners, chunks, PACK, 16, LANES), bf16),
            pltpu.VMEM((2, 8, lats, total), bf16),
            pltpu.VMEM((8, total, lats), bf16),
            pltpu.VMEM((2, lats, LANES), f32),
            pltpu.VMEM((2, bands, 8, 2, degrees, LANES), bf16),
            pltpu.VMEM((bands - 1, groups, 8, 2, degrees, LANES), bf16),
            pltpu.VMEM((2, 8, 2 * degrees, LANES), f32),
            dma((chunks, pairs)),
            dma((chunks, owners)),
            dma((chunks, owners)),
            dma((chunks,)),
            dma((groups, owners, pace + 1)),
            dma((groups, owners, pace + 1)),
            dma((groups,)),
            dma((groups,)),
            dma((groups, pace, bands)),
            dma((groups, pace, bands)),
            dma((groups, pace)),
        ],
        compiler_params=pltpu.CompilerParams(
            collective_id=0, has_side_effects=True, vmem_limit_bytes=VMEM_LIMIT
        ),
        cost_estimate=pl.CostEstimate(flops=8 * 10**9, bytes_accessed=40 * 10**6, transcendentals=0),
        name="chain",
    )(points, plan, order, band_filter, support, rooted, legendre)


def per_device_fused(
    control, vertical_root, legendre, band_filter, row_plan, wave_order, lat_points, support
):
    root = lax.dynamic_index_in_dim(vertical_root, row_plan[0, 0], 0, keepdims=False)
    rooted = jnp.einsum(
        "jik,kl->jil", control[0], root, preferred_element_type=jnp.float32
    ).astype(jnp.bfloat16)
    bands = lax.axis_size("band")
    result = chain(
        lat_points,
        row_plan,
        wave_order,
        band_filter,
        support.T,
        rooted,
        legendre,
        lax.axis_size("col"),
        bands,
    )
    slot_count, _, total = legendre.shape
    return result.reshape(slot_count, total // bands, 2, LANES)


def per_device(control, vertical_root, legendre, *rest):
    owners, bands = lax.axis_size("col"), lax.axis_size("band")
    _, lon_local, lats, _ = control.shape
    slot_count, _, total = legendre.shape
    chunks = lats // owners // 8
    fits = (
        vertical_root.shape[2] == LANES
        and lats % (16 * owners // math.gcd(owners, 2)) == 0
        and lats % (8 * owners) == 0
        and owners % 2 == 0
        and chunks % 2 == 1
        and lon_local % 16 == 0
        and (owners * lon_local) % LANES == 0
        and chunks >= 3
        and slot_count % 8 == 0
        and slot_count >= 24
        and (slot_count // 8 * owners) % 8 == 0
        and total % bands == 0
        and (total // bands) % 16 == 0
        and bands > 1
    )
    body = per_device_fused if fits else per_device_plain
    return body(control, vertical_root, legendre, *rest)


def solution(mesh):
    in_specs = (
        P("band", "col", None, None),
        P(),
        P("col", None, None),
        P(),
        P("band", None),
        P(),
        P("col"),
        P(),
    )
    out_specs = P("col", "band", None, None)
    return jax.shard_map(
        per_device, mesh=mesh, in_specs=in_specs, out_specs=out_specs, check_vma=False
    )
```

```python
import functools
import math

import jax
import jax.numpy as jnp
from jax import lax
from jax.experimental import pallas as pl
from jax.experimental.pallas import tpu as pltpu
from jax.sharding import PartitionSpec as P

LVR = 112
CHUNKS = (2, 2, 1)
LANES = 128
GROUP = 16
DEPTH = 2
VMEM_LIMIT = 58 * 2**20
PACK = LVR // GROUP
MESH = pl.DeviceIdType.MESH


def sine(theta):
    square = theta * theta
    value = -1.0 / 39916800.0 * square + 1.0 / 362880.0
    value = value * square - 1.0 / 5040.0
    value = value * square + 1.0 / 120.0
    value = value * square - 1.0 / 6.0
    value = value * square + 1.0
    return value * theta


def weights_kernel(points_ref, wave_ref, *out_refs):
    count = jnp.full((1, 1), points_ref[pl.program_id(0)], jnp.int32).astype(jnp.float32)
    lons = out_refs[0].shape[2]
    lanes = 128
    lon = lax.broadcasted_iota(jnp.int32, (1, lons), 1).astype(jnp.float32)
    full = 4.0 * count
    inverse = 1.0 / full
    unit = (2.0 * math.pi) * inverse
    scale = jnp.where(lon < count, lax.rsqrt(count), 0.0)
    nearest = 1.5 * 2.0**23
    first = 0
    for out_ref in out_refs:
        half = out_ref.shape[1] // 2
        tile = 8 if half % 16 else 16

        def rows(k, carry, out_ref=out_ref, first=first, tile=tile, half=half):
            at = pl.multiple_of(k * tile, tile)
            turns = wave_ref[pl.ds(first + at, tile), :] * lon[:, :lanes]
            whole = (turns * inverse + nearest) - nearest
            rest = turns - whole * full
            cos = sine((count - jnp.abs(rest)) * unit)
            away = jnp.abs(rest - count)
            sin = sine((count - jnp.minimum(away, full - away)) * unit)
            middle = lanes // 2
            cos_half = jnp.broadcast_to(cos[:, middle : middle + 1], cos.shape)
            sin_half = jnp.broadcast_to(sin[:, middle : middle + 1], sin.shape)
            cos_step = cos_half * cos_half - sin_half * sin_half
            sin_step = 2.0 * (cos_half * sin_half)
            for lo in range(0, lons, lanes):
                if lo:
                    cos, sin = (
                        cos * cos_step - sin * sin_step,
                        sin * cos_step + cos * sin_step,
                    )
                part = scale[:, lo : lo + lanes]
                out_ref[0, pl.ds(at, tile), lo : lo + lanes] = (cos * part).astype(
                    jnp.bfloat16
                )
                out_ref[0, pl.ds(half + at, tile), lo : lo + lanes] = (-sin * part).astype(
                    jnp.bfloat16
                )
            return carry

        lax.fori_loop(0, half // tile, rows, 0)
        first += half


def dft_weights(points, chunks, lon_count):
    lats = points.shape[0]
    shapes = [(lats, 2 * waves.size, lon_count) for waves in chunks]
    wave = jnp.concatenate([waves.reshape(-1) for waves in chunks])
    wave = 4.0 * wave.astype(jnp.float32)[:, None]
    return pl.pallas_call(
        weights_kernel,
        grid_spec=pltpu.PrefetchScalarGridSpec(
            num_scalar_prefetch=1,
            grid=(lats,),
            in_specs=[pl.BlockSpec(wave.shape, lambda i, p: (0, 0))],
            out_specs=[pl.BlockSpec((1,) + sh[1:], lambda i, p: (i, 0, 0)) for sh in shapes],
        ),
        out_shape=[jax.ShapeDtypeStruct(sh, jnp.bfloat16) for sh in shapes],
        cost_estimate=pl.CostEstimate(
            flops=20 * lats * wave.shape[0] * lon_count,
            bytes_accessed=4 * lats * wave.shape[0] * lon_count,
            transcendentals=0,
        ),
        name="weights",
    )(points, wave)


def dft_kernel(weight_ref, grid_ref, out_ref):
    lons = grid_ref.shape[0] * grid_ref.shape[2]
    owners, _, parts, slots, levels = out_ref.shape
    half = owners * slots
    for i in range(grid_ref.shape[1]):
        column = grid_ref[:, i].reshape(lons, levels)
        result = jnp.dot(weight_ref[i], column, preferred_element_type=jnp.float32)
        for p in range(parts):
            piece = result[p * half : (p + 1) * half].reshape(owners, slots, levels)
            out_ref[:, i, p] = piece.astype(jnp.bfloat16)


def dft(weights, grid_field, owners):
    lats, cols, lons = weights.shape
    ranks, _, lon_local, levels = grid_field.shape
    slots = cols // (2 * owners)
    block = max(d for d in range(1, 9) if lats % d == 0)
    return pl.pallas_call(
        dft_kernel,
        grid=(lats // block,),
        in_specs=[
            pl.BlockSpec((block, cols, lons), lambda i: (i, 0, 0)),
            pl.BlockSpec((ranks, block, lon_local, levels), lambda i: (0, i, 0, 0)),
        ],
        out_specs=pl.BlockSpec((owners, block, 2, slots, levels), lambda i: (0, i, 0, 0, 0)),
        out_shape=jax.ShapeDtypeStruct((owners, lats, 2, slots, levels), jnp.bfloat16),
        cost_estimate=pl.CostEstimate(
            flops=2 * lats * cols * lons * levels,
            bytes_accessed=2 * lats * (cols * lons + (cols + lons) * levels),
            transcendentals=0,
        ),
        name="dft",
    )(weights, grid_field)


def per_device_plain(
    control, vertical_root, legendre, band_filter, row_plan, wave_order, lat_points, support
):
    owners = lax.axis_size("col")
    band_id = row_plan[0, 0]
    level_start = row_plan[0, 1]
    root_band = lax.dynamic_index_in_dim(vertical_root, band_id, 0, keepdims=False)
    level = jnp.arange(root_band.shape[1], dtype=jnp.int32)
    inside = (level >= level_start) & (level < level_start + LVR)
    root_block = jnp.where(inside[None, :], root_band, jnp.zeros_like(root_band))
    columns = control[0]
    lon_local, lat_count, _ = columns.shape
    rooted = jnp.einsum(
        "jik,kl->ijl", columns, root_block, preferred_element_type=jnp.float32
    ).astype(jnp.bfloat16)
    rooted = rooted.reshape(owners, lat_count // owners, lon_local, -1)
    grid_field = lax.all_to_all(rooted, "col", split_axis=0, concat_axis=0, tiled=True)
    lon_count = lon_local * owners
    lat_local = lat_count // owners

    slot_count = legendre.shape[0]
    degree_count = legendre.shape[2]
    ends = [slot_count * sum(CHUNKS[: c + 1]) // sum(CHUNKS) for c in range(len(CHUNKS))]
    spans = list(zip([0] + ends[:-1], ends))
    waves = wave_order.reshape(owners, slot_count)
    owned_waves = lax.dynamic_index_in_dim(waves, lax.axis_index("col"), 0, keepdims=False)
    degree = jnp.arange(degree_count, dtype=jnp.int32)
    bounds = lax.dynamic_index_in_dim(support, band_id, 0, keepdims=False)
    filter_row = lax.dynamic_index_in_dim(band_filter, band_id, 0, keepdims=False)
    window = filter_row * ((degree >= bounds[0]) & (degree < bounds[1])).astype(jnp.float32)

    weights = dft_weights(lat_points, [waves[:, lo:hi] for lo, hi in spans], lon_count)
    outputs = []
    fourier = dft(weights[0], grid_field, owners)
    for c, (lo, hi) in enumerate(spans):
        owned = lax.all_to_all(fourier, "col", split_axis=0, concat_axis=0, tiled=True)
        if c + 1 < len(spans):
            fourier = dft(weights[c + 1], grid_field, owners)
        if c:
            fourier, owned, _ = lax.optimization_barrier((fourier, owned, contribution))
        else:
            fourier, owned = lax.optimization_barrier((fourier, owned))
        owned = owned.reshape(lat_count, 2, hi - lo, owned.shape[4])
        spectral = jnp.einsum(
            "xpsl,sxn->snpl",
            owned,
            legendre[lo:hi],
            preferred_element_type=jnp.float32,
        )
        spectral_weight = (degree[None, :] >= owned_waves[lo:hi][:, None]).astype(
            jnp.float32
        ) * window[None, :]
        contribution = (spectral * spectral_weight[:, :, None, None]).astype(jnp.bfloat16)
        if c:
            contribution, outputs[-1] = lax.optimization_barrier((contribution, outputs[-1]))
        outputs.append(
            lax.psum_scatter(contribution, "band", scatter_dimension=1, tiled=True)
        )
    return jnp.concatenate(outputs, axis=0).astype(jnp.float32)


def greet(axes):
    barrier = pltpu.get_barrier_semaphore()
    total = 0
    for axis in axes:
        size, me = lax.axis_size(axis), lax.axis_index(axis)
        for d in range(1, size):
            pl.semaphore_signal(
                barrier,
                inc=1,
                device_id={axis: lax.rem(me + d, size)},
                device_id_type=MESH,
            )
        total += size - 1
    pl.semaphore_wait(barrier, total)


def lat_weights(count, wave_ref, lons, out_ref, index, tile):
    full = 4.0 * count
    inverse = 1.0 / full
    unit = (2.0 * math.pi) * inverse
    lon = lax.broadcasted_iota(jnp.int32, (1, lons), 1).astype(jnp.float32)
    scale = jnp.where(lon < count, lax.rsqrt(count), 0.0)
    nearest = 1.5 * 2.0**23
    half = wave_ref.shape[0]

    def rows(k, carry):
        at = pl.multiple_of(k * tile, tile)
        turns = wave_ref[pl.ds(at, tile), :] * lon[:, :LANES]
        whole = (turns * inverse + nearest) - nearest
        rest = turns - whole * full
        cos = sine((count - jnp.abs(rest)) * unit)
        away = jnp.abs(rest - count)
        sin = sine((jnp.minimum(away, full - away) - count) * unit)
        middle = LANES // 2
        cos_half = jnp.broadcast_to(cos[:, middle : middle + 1], cos.shape)
        sin_half = jnp.broadcast_to(sin[:, middle : middle + 1], sin.shape)
        cos_step = cos_half * cos_half - sin_half * sin_half
        sin_step = 2.0 * (cos_half * sin_half)
        for lo in range(0, lons, LANES):
            if lo:
                cos, sin = (
                    cos * cos_step - sin * sin_step,
                    sin * cos_step + cos * sin_step,
                )
            part = scale[:, lo : lo + LANES]
            out_ref[index, pl.ds(at, tile), lo : lo + LANES] = (cos * part).astype(
                jnp.bfloat16
            )
            out_ref[index, pl.ds(half + at, tile), lo : lo + LANES] = (
                sin * part
            ).astype(jnp.bfloat16)
        return carry

    lax.fori_loop(0, half // tile, rows, 0)


def lat_tiles(lats):
    return [(lo, min(LANES, lats - lo)) for lo in range(0, lats, LANES)]


def lat_chunks(lats, owners):
    out = []
    for n, (lo, width) in enumerate(lat_tiles(lats)):
        step = width // owners
        out += [(lo + at, step, n) for at in range(0, step, 8)]
    return out


def chain_kernel(
    points_ref,
    plan_ref,
    order_ref,
    filter_ref,
    support_ref,
    root_ref,
    control_ref,
    legendre_ref,
    out_ref,
    wave,
    window,
    points,
    control,
    planes,
    rows_of,
    sent,
    got,
    weight,
    turned,
    fourier,
    owned,
    leg,
    leg_t,
    last,
    part,
    other,
    points_sem,
    points_got_sem,
    control_sem,
    send_sem,
    recv_sem,
    own_sem,
    send2_sem,
    recv2_sem,
    own2_sem,
    leg_sem,
    part_sem,
    other_sem,
):
    chunks, owners, _, lon_local, _ = sent.shape
    groups = fourier.shape[0]
    bands, _, _, degrees, _ = part.shape[1:]
    lons = owners * lon_local
    lats = owners * chunks * 8
    waves, total = wave.shape[0], window.shape[0]
    eighth = waves // 8
    early = chunks - 1
    plan = lat_chunks(lats, owners)
    pace = part_sem.shape[1]
    run = 8 // pace
    me, band = lax.axis_index("col"), lax.axis_index("band")

    lane = lax.broadcasted_iota(jnp.int32, (1, LANES), 1)
    rel = lane - plan_ref[0, 1]
    rel = jnp.where(rel < 0, rel + LANES, rel)
    spare = rel >= LVR

    def load_control(t):
        at = pl.multiple_of(16 * t, 16)
        return pltpu.make_async_copy(
            control_ref.at[:, pl.ds(at, 16), :], control.at[t], control_sem.at[t]
        )

    def across(src, dst, send, recv, to):
        return pltpu.make_async_remote_copy(
            src_ref=src,
            dst_ref=dst,
            send_sem=send,
            recv_sem=recv,
            device_id={"col": to},
            device_id_type=MESH,
        )

    def grid_copy(k, d):
        to = lax.rem(me + d, owners)
        return across(
            sent.at[k, to], got.at[k, me], send_sem.at[k, d], recv_sem.at[k, d], to
        )

    def points_copy(d):
        to = lax.rem(me + d, owners)
        return across(
            points_ref, points.at[me], points_sem.at[d], points_got_sem.at[d], to
        )

    points_own = pltpu.make_async_copy(points_ref, points.at[me], points_sem.at[0])

    def grid_own(k):
        return pltpu.make_async_copy(sent.at[k, me], got.at[k, me], own_sem.at[k])

    def grid_send(k):
        for d in range(1, owners):
            grid_copy(k, d).start()
        grid_own(k).start()

    def view(ref, c, dev, piece):
        if piece == "late":
            return ref.at[c, dev, pl.ds(early, 1)]
        first = piece % pace * run
        tiles = pl.ds(first, min(run, PACK - first))
        if piece >= pace:
            return ref.at[c, dev, pl.ds(0, early), tiles]
        return ref.at[c, dev, :, tiles]

    def wave_copy(c, d, piece):
        to = lax.rem(me + d, owners)
        e = pace if piece == "late" else piece % pace
        return across(
            view(fourier, c, to, piece),
            view(owned, c, me, piece),
            send2_sem.at[c, d, e],
            recv2_sem.at[c, d, e],
            to,
        )

    def wave_own(c):
        return pltpu.make_async_copy(fourier.at[c, me], owned.at[c, me], own2_sem.at[c])

    def wave_start(c, piece):
        for d in range(1, owners):
            wave_copy(c, d, piece).start()

    def wave_wait(c, piece):
        for d in range(1, owners):
            wave_copy(c, d, piece).wait()

    def load_leg(c):
        at = pl.multiple_of(8 * c, 8)
        return pltpu.make_async_copy(
            legendre_ref.at[pl.ds(at, 8)], leg.at[lax.rem(c, 2)], leg_sem.at[c]
        )

    def give(c, h, d):
        to = lax.rem(band + d, bands)
        return pltpu.make_async_remote_copy(
            src_ref=part.at[lax.rem(c, 2), to, pl.ds(run * h, run)],
            dst_ref=other.at[d - 1, c, pl.ds(run * h, run)],
            send_sem=part_sem.at[c, h, d],
            recv_sem=other_sem.at[c, h, d],
            device_id={"band": to},
            device_id_type=MESH,
        )

    for t in range(control.shape[0]):
        load_control(t).start()
    points_own.start()
    greet(["col", "band"])
    for d in range(1, owners):
        points_copy(d).start()

    band_id = plan_ref[0, 0]
    root = root_ref[0]
    for b in range(1, root_ref.shape[0]):
        here = jnp.full(root.shape, band_id, jnp.int32) == b
        root = jnp.where(here, root_ref[b].astype(jnp.float32), root.astype(jnp.float32))
        root = root.astype(jnp.bfloat16)
    levels = root.shape[0]

    for n, (lo, width) in enumerate(lat_tiles(lats)):

        def root_tile(t, carry, n=n, lo=lo, width=width):
            if n == 0:
                load_control(t).wait()
            values = control[t, :, :, lo : lo + width].astype(jnp.float32)
            planes[:, :width] = values.reshape(levels * 16, width)
            for j in range(16):
                plane = planes[pl.ds(j, levels, stride=16), :][:, :width]
                rooted = lax.dot_general(
                    plane.astype(jnp.bfloat16),
                    root,
                    (((0,), (0,)), ((), ())),
                    preferred_element_type=jnp.float32,
                )
                rows_of[pl.ds(j, width, stride=16), :] = rooted
            at = pl.multiple_of(16 * t, 16)
            for k, (first, step, tile) in enumerate(plan):
                if tile != n:
                    continue

                def owner(to, c, k=k, first=first, step=step):
                    start = pl.multiple_of((first - lo + step * to) * 16, 128)
                    extra = rows_of[pl.ds(start + 16 * PACK, 16), :]
                    for g in range(PACK):
                        mine = rows_of[pl.ds(start + 16 * g, 16), :]
                        moved = pltpu.roll(extra, LVR - GROUP * g, 1)
                        value = jnp.where(spare, moved, mine).astype(jnp.bfloat16)
                        sent[k, to, g, pl.ds(at, 16), :] = value
                    return c

                lax.fori_loop(0, owners, owner, 0)
            return carry

        lax.fori_loop(0, control.shape[0], root_tile, 0)
        if n == 0:
            for k in range(2):
                grid_send(k)
            for c in range(2):
                load_leg(c).start()
    for d in range(1, owners):
        points_copy(d).wait()
    points_own.wait()

    def wave_row(r, carry):
        sl, rest = r // eighth, lax.rem(r, eighth)
        c, dev = rest // owners, lax.rem(rest, owners)
        value = order_ref[dev * (8 * groups) + 8 * c + sl]
        wave[pl.ds(r, 1), :] = jnp.full((1, LANES), 4 * value, jnp.int32).astype(jnp.float32)
        return carry

    lax.fori_loop(0, waves, wave_row, 0)
    lower, upper = support_ref[0, band_id], support_ref[1, band_id]

    def window_row(n, carry):
        row = jnp.full((1, LANES), filter_ref[band_id, n], jnp.float32)
        at = jnp.full((1, LANES), n, jnp.int32)
        live = (at >= lower) & (at < upper) & (rel < LVR)
        window[pl.ds(n, 1), :] = jnp.where(live, row, 0.0)
        return carry

    lax.fori_loop(0, total, window_row, 0)

    def transform(k, lat, x):
        for p in range(2):
            res = jnp.dot(
                weight[lat, p * waves : (p + 1) * waves, :],
                x,
                preferred_element_type=jnp.float32,
            )
            extra = res[PACK * eighth :]
            for g in range(PACK):
                moved = pltpu.roll(extra, LVR - GROUP * g, 1)
                piece = jnp.where(spare, moved, res[g * eighth : (g + 1) * eighth])
                turned[pl.ds(g * eighth * 16 + p * 8 + lat, eighth, stride=16), :] = piece

    def chunk(k, carry):
        first, step = jnp.int32(0), jnp.int32(0)
        for i, (lo, by, _) in enumerate(plan):
            first = jnp.where(k == i, lo, first)
            step = jnp.where(k == i, by, step)

        def make(lat, c):
            index = first + step * me + lat
            held = lats // owners
            row = points[index // held].astype(jnp.float32)
            column = lax.broadcasted_iota(jnp.int32, row.shape, 1)
            row = jnp.where(column == lax.rem(index, held), row, 0.0)
            count = jnp.sum(row, axis=1, keepdims=True)
            lat_weights(count, wave, lons, weight, lat, 32 if waves % 32 == 0 else 8)
            return c

        lax.fori_loop(0, 8, make, 0)
        for d in range(1, owners):
            grid_copy(k, d).wait()
        grid_own(k).wait()

        @pl.when(k + 2 < chunks)
        def _():
            grid_send(k + 2)

        @pl.when(k == chunks - 1)
        def _():
            for q in range(1, pace):
                wave_start(0, pace + q)

        def plain(g, c):
            transform(k, g, got[k, :, g].reshape(lons, LANES))
            return c

        lax.fori_loop(0, PACK, plain, 0)
        x = jnp.zeros((lons, LANES), jnp.float32)
        for g in range(PACK):
            moved = got[k, :, g].reshape(lons, LANES).astype(jnp.float32)
            moved = pltpu.roll(moved, LANES - LVR + GROUP * g, 1)
            x = jnp.where((rel >= GROUP * g) & (rel < GROUP * (g + 1)), moved, x)
        transform(k, PACK, x.astype(jnp.bfloat16))
        for c in range(groups):
            for g in range(PACK):
                at = (g * eighth + c * owners) * 16
                rows = turned[at : at + 16 * owners, :].reshape(owners, 16, LANES)
                fourier[c, :, k, g] = rows.astype(jnp.bfloat16)

        @pl.when(k == early - 1)
        def _():
            wave_start(0, pace)

        return carry

    lax.fori_loop(0, chunks, chunk, 0)
    wave_start(0, "late")
    wave_own(0).start()
    for q in range(DEPTH):
        wave_start(1, q)
    wave_own(1).start()

    tiles = [
        [k for k, entry in enumerate(plan) if entry[2] == n]
        for n in range(len(lat_tiles(lats)))
    ]

    def finish(c):
        for h in range(pace):
            for d in range(1, bands):
                give(c, h, d).wait_recv()
            for sl in range(run * h, run * (h + 1)):
                for p in range(2):
                    acc = part[lax.rem(c, 2), band, sl, p].astype(jnp.float32)
                    for d in range(1, bands):
                        acc = acc + other[d - 1, c, sl, p].astype(jnp.float32)
                    out_ref[8 * c + sl, pl.ds(p, degrees, stride=2), :] = acc

    def slot_out(c, sl, halves):
        res = jnp.dot(
            leg_t[sl],
            jnp.concatenate([h.astype(jnp.bfloat16) for h in halves], axis=1),
            preferred_element_type=jnp.float32,
        )
        degree = lax.broadcasted_iota(jnp.int32, (total, LANES), 0)
        order_here = order_ref[me * (8 * groups) + 8 * c + sl]
        keep = jnp.where(degree >= order_here, window[...], 0.0)
        for p in range(2):
            value = (res[:, p * LANES : (p + 1) * LANES] * keep).astype(jnp.bfloat16)
            part[lax.rem(c, 2), :, sl, p] = value.reshape(bands, degrees, LANES)
        if sl % run == run - 1:
            for d in range(1, bands):
                give(c, sl // run, d).start()

    def group(c, carry):
        load_leg(c).wait()
        for sl in range(8):
            leg_t[sl] = leg[lax.rem(c, 2), sl].T

        @pl.when(c + 2 < groups)
        def _():
            load_leg(c + 2).start()

        def arrive(q):
            @pl.when(c == 0)
            def _():
                wave_wait(0, pace + q)
                if q == 0:
                    wave_wait(0, "late")

            @pl.when(c > 0)
            def _():
                wave_wait(c, q)
                if q + DEPTH < pace:
                    wave_start(c, q + DEPTH)

            @pl.when((c > 0) & (c + 1 < groups))
            def _():
                if q + DEPTH >= pace:
                    wave_start(c + 1, q + DEPTH - pace)

        arrive(0)
        wave_own(c).wait()

        @pl.when(c + 2 < groups)
        def _():
            wave_own(c + 2).start()

        @pl.when(c >= 2)
        def _():
            for h in range(pace):
                for d in range(1, bands):
                    give(c - 2, h, d).wait_send()

        for sl in range(PACK):
            if sl and sl % run == 0:
                arrive(sl // run)
            value = [
                owned[c, :, tile[0] : tile[-1] + 1, sl].astype(jnp.float32)
                for tile in tiles
            ]
            value = [v.reshape(-1, 2, 8, LANES) for v in value]
            value = jnp.concatenate(value, axis=0)
            halves = [value[:, p].reshape(lats, LANES) for p in range(2)]
            here = (rel >= GROUP * sl) & (rel < GROUP * (sl + 1))
            for p in range(2):
                moved = pltpu.roll(halves[p], LANES - LVR + GROUP * sl, 1)
                before = last[p] if sl else jnp.zeros((lats, LANES), jnp.float32)
                last[p] = jnp.where(here, moved, before)
            slot_out(c, sl, halves)
        slot_out(c, PACK, [last[0], last[1]])

        @pl.when(c >= 1)
        def _():
            finish(c - 1)

        return carry

    lax.fori_loop(0, groups, group, 0)
    finish(groups - 1)
    for c in range(groups - 2, groups):
        for h in range(pace):
            for d in range(1, bands):
                give(c, h, d).wait_send()


def chain(points, plan, order, band_filter, support, root, control, legendre, owners, bands):
    levels, lon_local, lats = control.shape
    slot_count, _, total = legendre.shape
    waves = order.shape[0]
    chunks, groups = lats // owners // 8, slot_count // 8
    lons, degrees, pace = owners * lon_local, total // bands, 4
    bf16, f32 = jnp.bfloat16, jnp.float32
    any_spec = pl.BlockSpec(memory_space=pl.ANY)
    smem_spec = pl.BlockSpec(memory_space=pltpu.SMEM)
    vmem_spec = pl.BlockSpec(memory_space=pltpu.VMEM)
    dma = pltpu.SemaphoreType.DMA
    return pl.pallas_call(
        chain_kernel,
        in_specs=[any_spec] + [smem_spec] * 4 + [vmem_spec, any_spec, any_spec],
        out_specs=vmem_spec,
        out_shape=pltpu.VMEM((slot_count, 2 * degrees, LANES), f32),
        scratch_shapes=[
            pltpu.VMEM((waves, LANES), f32),
            pltpu.VMEM((total, LANES), f32),
            pltpu.VMEM((owners, 1, lats // owners), jnp.int32),
            pltpu.VMEM((lon_local // 16, levels, 16, lats), bf16),
            pltpu.VMEM((levels * 16, LANES), f32),
            pltpu.VMEM((16 * LANES, LANES), f32),
            pltpu.VMEM((chunks, owners, PACK, lon_local, LANES), bf16),
            pltpu.VMEM((chunks, owners, PACK, lon_local, LANES), bf16),
            pltpu.VMEM((8, 2 * waves, lons), bf16),
            pltpu.VMEM((PACK * waves // 8 * 16, LANES), f32),
            pltpu.VMEM((groups, owners, chunks, PACK, 16, LANES), bf16),
            pltpu.VMEM((groups, owners, chunks, PACK, 16, LANES), bf16),
            pltpu.VMEM((2, 8, lats, total), bf16),
            pltpu.VMEM((8, total, lats), bf16),
            pltpu.VMEM((2, lats, LANES), f32),
            pltpu.VMEM((2, bands, 8, 2, degrees, LANES), bf16),
            pltpu.VMEM((bands - 1, groups, 8, 2, degrees, LANES), bf16),
            dma((owners,)),
            dma((owners,)),
            dma((lon_local // 16,)),
            dma((chunks, owners)),
            dma((chunks, owners)),
            dma((chunks,)),
            dma((groups, owners, pace + 1)),
            dma((groups, owners, pace + 1)),
            dma((groups,)),
            dma((groups,)),
            dma((groups, pace, bands)),
            dma((groups, pace, bands)),
        ],
        compiler_params=pltpu.CompilerParams(
            collective_id=0, has_side_effects=True, vmem_limit_bytes=VMEM_LIMIT
        ),
        cost_estimate=pl.CostEstimate(flops=8 * 10**9, bytes_accessed=40 * 10**6, transcendentals=0),
        name="chain",
    )(points, plan, order, band_filter, support, root, control, legendre)


def per_device_fused(
    control, vertical_root, legendre, band_filter, row_plan, wave_order, lat_points, support
):
    bands = lax.axis_size("band")
    result = chain(
        lat_points[None, :],
        row_plan,
        wave_order,
        band_filter,
        support.T,
        vertical_root,
        control[0].transpose(2, 0, 1),
        legendre,
        lax.axis_size("col"),
        bands,
    )
    slot_count, _, total = legendre.shape
    return result.reshape(slot_count, total // bands, 2, LANES)


def per_device(control, vertical_root, legendre, *rest):
    owners, bands = lax.axis_size("col"), lax.axis_size("band")
    _, lon_local, lats, _ = control.shape
    slot_count, _, total = legendre.shape
    chunks = lats // owners // 8
    fits = (
        vertical_root.shape[2] == LANES
        and all(width % (8 * owners) == 0 for _, width in lat_tiles(lats))
        and lats % (8 * owners) == 0
        and lon_local % 16 == 0
        and (owners * lon_local) % LANES == 0
        and chunks >= 3
        and slot_count % 8 == 0
        and slot_count >= 24
        and (slot_count // 8 * owners) % 8 == 0
        and total % bands == 0
        and (total // bands) % 16 == 0
        and bands > 1
    )
    body = per_device_fused if fits else per_device_plain
    return body(control, vertical_root, legendre, *rest)


def solution(mesh):
    in_specs = (
        P("band", "col", None, None),
        P(),
        P("col", None, None),
        P(),
        P("band", None),
        P(),
        P("col"),
        P(),
    )
    out_specs = P("col", "band", None, None)
    return jax.shard_map(
        per_device, mesh=mesh, in_specs=in_specs, out_specs=out_specs, check_vma=False
    )
```

```python
import functools
import math

import jax
import jax.numpy as jnp
from jax import lax
from jax.experimental import pallas as pl
from jax.experimental.pallas import tpu as pltpu
from jax.sharding import PartitionSpec as P

LVR = 112
CHUNKS = (2, 2, 1)
LANES = 128
GROUP = 16
DEPTH = 2
VMEM_LIMIT = 58 * 2**20
PACK = LVR // GROUP
MESH = pl.DeviceIdType.MESH


def sine(theta):
    square = theta * theta
    value = -1.0 / 39916800.0 * square + 1.0 / 362880.0
    value = value * square - 1.0 / 5040.0
    value = value * square + 1.0 / 120.0
    value = value * square - 1.0 / 6.0
    value = value * square + 1.0
    return value * theta


def weights_kernel(points_ref, wave_ref, *out_refs):
    count = jnp.full((1, 1), points_ref[pl.program_id(0)], jnp.int32).astype(jnp.float32)
    lons = out_refs[0].shape[2]
    lanes = 128
    lon = lax.broadcasted_iota(jnp.int32, (1, lons), 1).astype(jnp.float32)
    full = 4.0 * count
    inverse = 1.0 / full
    unit = (2.0 * math.pi) * inverse
    scale = jnp.where(lon < count, lax.rsqrt(count), 0.0)
    nearest = 1.5 * 2.0**23
    first = 0
    for out_ref in out_refs:
        half = out_ref.shape[1] // 2
        tile = 8 if half % 16 else 16

        def rows(k, carry, out_ref=out_ref, first=first, tile=tile, half=half):
            at = pl.multiple_of(k * tile, tile)
            turns = wave_ref[pl.ds(first + at, tile), :] * lon[:, :lanes]
            whole = (turns * inverse + nearest) - nearest
            rest = turns - whole * full
            cos = sine((count - jnp.abs(rest)) * unit)
            away = jnp.abs(rest - count)
            sin = sine((count - jnp.minimum(away, full - away)) * unit)
            middle = lanes // 2
            cos_half = jnp.broadcast_to(cos[:, middle : middle + 1], cos.shape)
            sin_half = jnp.broadcast_to(sin[:, middle : middle + 1], sin.shape)
            cos_step = cos_half * cos_half - sin_half * sin_half
            sin_step = 2.0 * (cos_half * sin_half)
            for lo in range(0, lons, lanes):
                if lo:
                    cos, sin = (
                        cos * cos_step - sin * sin_step,
                        sin * cos_step + cos * sin_step,
                    )
                part = scale[:, lo : lo + lanes]
                out_ref[0, pl.ds(at, tile), lo : lo + lanes] = (cos * part).astype(
                    jnp.bfloat16
                )
                out_ref[0, pl.ds(half + at, tile), lo : lo + lanes] = (-sin * part).astype(
                    jnp.bfloat16
                )
            return carry

        lax.fori_loop(0, half // tile, rows, 0)
        first += half


def dft_weights(points, chunks, lon_count):
    lats = points.shape[0]
    shapes = [(lats, 2 * waves.size, lon_count) for waves in chunks]
    wave = jnp.concatenate([waves.reshape(-1) for waves in chunks])
    wave = 4.0 * wave.astype(jnp.float32)[:, None]
    return pl.pallas_call(
        weights_kernel,
        grid_spec=pltpu.PrefetchScalarGridSpec(
            num_scalar_prefetch=1,
            grid=(lats,),
            in_specs=[pl.BlockSpec(wave.shape, lambda i, p: (0, 0))],
            out_specs=[pl.BlockSpec((1,) + sh[1:], lambda i, p: (i, 0, 0)) for sh in shapes],
        ),
        out_shape=[jax.ShapeDtypeStruct(sh, jnp.bfloat16) for sh in shapes],
        cost_estimate=pl.CostEstimate(
            flops=20 * lats * wave.shape[0] * lon_count,
            bytes_accessed=4 * lats * wave.shape[0] * lon_count,
            transcendentals=0,
        ),
        name="weights",
    )(points, wave)


def dft_kernel(weight_ref, grid_ref, out_ref):
    lons = grid_ref.shape[0] * grid_ref.shape[2]
    owners, _, parts, slots, levels = out_ref.shape
    half = owners * slots
    for i in range(grid_ref.shape[1]):
        column = grid_ref[:, i].reshape(lons, levels)
        result = jnp.dot(weight_ref[i], column, preferred_element_type=jnp.float32)
        for p in range(parts):
            piece = result[p * half : (p + 1) * half].reshape(owners, slots, levels)
            out_ref[:, i, p] = piece.astype(jnp.bfloat16)


def dft(weights, grid_field, owners):
    lats, cols, lons = weights.shape
    ranks, _, lon_local, levels = grid_field.shape
    slots = cols // (2 * owners)
    block = max(d for d in range(1, 9) if lats % d == 0)
    return pl.pallas_call(
        dft_kernel,
        grid=(lats // block,),
        in_specs=[
            pl.BlockSpec((block, cols, lons), lambda i: (i, 0, 0)),
            pl.BlockSpec((ranks, block, lon_local, levels), lambda i: (0, i, 0, 0)),
        ],
        out_specs=pl.BlockSpec((owners, block, 2, slots, levels), lambda i: (0, i, 0, 0, 0)),
        out_shape=jax.ShapeDtypeStruct((owners, lats, 2, slots, levels), jnp.bfloat16),
        cost_estimate=pl.CostEstimate(
            flops=2 * lats * cols * lons * levels,
            bytes_accessed=2 * lats * (cols * lons + (cols + lons) * levels),
            transcendentals=0,
        ),
        name="dft",
    )(weights, grid_field)


def per_device_plain(
    control, vertical_root, legendre, band_filter, row_plan, wave_order, lat_points, support
):
    owners = lax.axis_size("col")
    band_id = row_plan[0, 0]
    level_start = row_plan[0, 1]
    root_band = lax.dynamic_index_in_dim(vertical_root, band_id, 0, keepdims=False)
    level = jnp.arange(root_band.shape[1], dtype=jnp.int32)
    inside = (level >= level_start) & (level < level_start + LVR)
    root_block = jnp.where(inside[None, :], root_band, jnp.zeros_like(root_band))
    columns = control[0]
    lon_local, lat_count, _ = columns.shape
    rooted = jnp.einsum(
        "jik,kl->ijl", columns, root_block, preferred_element_type=jnp.float32
    ).astype(jnp.bfloat16)
    rooted = rooted.reshape(owners, lat_count // owners, lon_local, -1)
    grid_field = lax.all_to_all(rooted, "col", split_axis=0, concat_axis=0, tiled=True)
    lon_count = lon_local * owners
    lat_local = lat_count // owners

    slot_count = legendre.shape[0]
    degree_count = legendre.shape[2]
    ends = [slot_count * sum(CHUNKS[: c + 1]) // sum(CHUNKS) for c in range(len(CHUNKS))]
    spans = list(zip([0] + ends[:-1], ends))
    waves = wave_order.reshape(owners, slot_count)
    owned_waves = lax.dynamic_index_in_dim(waves, lax.axis_index("col"), 0, keepdims=False)
    degree = jnp.arange(degree_count, dtype=jnp.int32)
    bounds = lax.dynamic_index_in_dim(support, band_id, 0, keepdims=False)
    filter_row = lax.dynamic_index_in_dim(band_filter, band_id, 0, keepdims=False)
    window = filter_row * ((degree >= bounds[0]) & (degree < bounds[1])).astype(jnp.float32)

    weights = dft_weights(lat_points, [waves[:, lo:hi] for lo, hi in spans], lon_count)
    outputs = []
    fourier = dft(weights[0], grid_field, owners)
    for c, (lo, hi) in enumerate(spans):
        owned = lax.all_to_all(fourier, "col", split_axis=0, concat_axis=0, tiled=True)
        if c + 1 < len(spans):
            fourier = dft(weights[c + 1], grid_field, owners)
        if c:
            fourier, owned, _ = lax.optimization_barrier((fourier, owned, contribution))
        else:
            fourier, owned = lax.optimization_barrier((fourier, owned))
        owned = owned.reshape(lat_count, 2, hi - lo, owned.shape[4])
        spectral = jnp.einsum(
            "xpsl,sxn->snpl",
            owned,
            legendre[lo:hi],
            preferred_element_type=jnp.float32,
        )
        spectral_weight = (degree[None, :] >= owned_waves[lo:hi][:, None]).astype(
            jnp.float32
        ) * window[None, :]
        contribution = (spectral * spectral_weight[:, :, None, None]).astype(jnp.bfloat16)
        if c:
            contribution, outputs[-1] = lax.optimization_barrier((contribution, outputs[-1]))
        outputs.append(
            lax.psum_scatter(contribution, "band", scatter_dimension=1, tiled=True)
        )
    return jnp.concatenate(outputs, axis=0).astype(jnp.float32)


def greet(axes):
    barrier = pltpu.get_barrier_semaphore()
    total = 0
    for axis in axes:
        size, me = lax.axis_size(axis), lax.axis_index(axis)
        for d in range(1, size):
            pl.semaphore_signal(
                barrier,
                inc=1,
                device_id={axis: lax.rem(me + d, size)},
                device_id_type=MESH,
            )
        total += size - 1
    pl.semaphore_wait(barrier, total)


def lat_weights(count, wave_ref, lons, out_ref, index, tile):
    full = 4.0 * count
    inverse = 1.0 / full
    unit = (2.0 * math.pi) * inverse
    lon = lax.broadcasted_iota(jnp.int32, (1, lons), 1).astype(jnp.float32)
    scale = jnp.where(lon < count, lax.rsqrt(count), 0.0)
    nearest = 1.5 * 2.0**23
    half = wave_ref.shape[0]

    def rows(k, carry):
        at = pl.multiple_of(k * tile, tile)
        turns = wave_ref[pl.ds(at, tile), :] * lon[:, :LANES]
        whole = (turns * inverse + nearest) - nearest
        rest = turns - whole * full
        cos = sine((count - jnp.abs(rest)) * unit)
        away = jnp.abs(rest - count)
        sin = sine((jnp.minimum(away, full - away) - count) * unit)
        middle = LANES // 2
        cos_half = jnp.broadcast_to(cos[:, middle : middle + 1], cos.shape)
        sin_half = jnp.broadcast_to(sin[:, middle : middle + 1], sin.shape)
        cos_step = cos_half * cos_half - sin_half * sin_half
        sin_step = 2.0 * (cos_half * sin_half)
        for lo in range(0, lons, LANES):
            if lo:
                cos, sin = (
                    cos * cos_step - sin * sin_step,
                    sin * cos_step + cos * sin_step,
                )
            part = scale[:, lo : lo + LANES]
            out_ref[index, pl.ds(at, tile), lo : lo + LANES] = (cos * part).astype(
                jnp.bfloat16
            )
            out_ref[index, pl.ds(half + at, tile), lo : lo + LANES] = (
                sin * part
            ).astype(jnp.bfloat16)
        return carry

    lax.fori_loop(0, half // tile, rows, 0)


def lat_tiles(lats):
    return [(lo, min(LANES, lats - lo)) for lo in range(0, lats, LANES)]


def lat_chunks(lats, owners):
    out = []
    for n, (lo, width) in enumerate(lat_tiles(lats)):
        step = width // owners
        out += [(lo + at, step, n) for at in range(0, step, 8)]
    return out


def chain_kernel(
    points_ref,
    plan_any,
    order_any,
    filter_any,
    support_any,
    root_any,
    control_ref,
    legendre_ref,
    out_ref,
    plan_ref,
    order_ref,
    filter_ref,
    support_ref,
    root_ref,
    wave,
    window,
    points,
    control,
    planes,
    rows_of,
    sent,
    got,
    weight,
    turned,
    fourier,
    owned,
    leg,
    leg_t,
    last,
    part,
    other,
    points_sem,
    points_got_sem,
    control_sem,
    piece_sem,
    piece_got_sem,
    small_sem,
    send_sem,
    recv_sem,
    own_sem,
    send2_sem,
    recv2_sem,
    own2_sem,
    leg_sem,
    part_sem,
    other_sem,
):
    chunks, owners, _, lon_local, _ = sent.shape
    groups = fourier.shape[0]
    bands, _, _, degrees, _ = part.shape[1:]
    lons = owners * lon_local
    lats = owners * chunks * 8
    waves, total = wave.shape[0], window.shape[0]
    eighth = waves // 8
    early = chunks - 1
    plan = lat_chunks(lats, owners)
    pace = part_sem.shape[1]
    run = 8 // pace
    me, band = lax.axis_index("col"), lax.axis_index("band")

    small = [
        pltpu.make_async_copy(src, dst, small_sem.at[i])
        for i, (src, dst) in enumerate(
            [
                (plan_any, plan_ref),
                (root_any, root_ref),
                (order_any, order_ref),
                (filter_any, filter_ref),
                (support_any, support_ref),
            ]
        )
    ]
    for copy in small:
        copy.start()

    def load_control(t):
        at = pl.multiple_of(16 * t, 16)
        return pltpu.make_async_copy(
            control_ref.at[:, pl.ds(at, 16), :], control.at[t], control_sem.at[t]
        )

    def across(src, dst, send, recv, to):
        return pltpu.make_async_remote_copy(
            src_ref=src,
            dst_ref=dst,
            send_sem=send,
            recv_sem=recv,
            device_id={"col": to},
            device_id_type=MESH,
        )

    def grid_copy(k, d):
        to = lax.rem(me + d, owners)
        return across(
            sent.at[k, to], got.at[k, me], send_sem.at[k, d], recv_sem.at[k, d], to
        )

    def points_copy(d):
        to = lax.rem(me + d, owners)
        return across(
            points_ref, points.at[me], points_sem.at[d], points_got_sem.at[d], to
        )

    points_own = pltpu.make_async_copy(points_ref, points.at[me], points_sem.at[0])

    def piece_copy(t, d):
        to = lax.rem(me + d, owners)
        rows = pl.ds(pl.multiple_of(16 * t, 16), 16)
        return across(
            sent.at[0, to, :, rows],
            got.at[0, me, :, rows],
            piece_sem.at[t, d],
            piece_got_sem.at[t, d],
            to,
        )

    def grid_own(k):
        return pltpu.make_async_copy(sent.at[k, me], got.at[k, me], own_sem.at[k])

    def grid_send(k):
        for d in range(1, owners):
            grid_copy(k, d).start()
        grid_own(k).start()

    def view(ref, c, dev, piece):
        if piece == "late":
            return ref.at[c, dev, pl.ds(early, 1)]
        first = piece % pace * run
        tiles = pl.ds(first, min(run, PACK - first))
        if piece >= pace:
            return ref.at[c, dev, pl.ds(0, early), tiles]
        return ref.at[c, dev, :, tiles]

    def wave_copy(c, d, piece):
        to = lax.rem(me + d, owners)
        e = pace if piece == "late" else piece % pace
        return across(
            view(fourier, c, to, piece),
            view(owned, c, me, piece),
            send2_sem.at[c, d, e],
            recv2_sem.at[c, d, e],
            to,
        )

    def wave_own(c):
        return pltpu.make_async_copy(fourier.at[c, me], owned.at[c, me], own2_sem.at[c])

    def wave_start(c, piece):
        for d in range(1, owners):
            wave_copy(c, d, piece).start()

    def wave_wait(c, piece):
        for d in range(1, owners):
            wave_copy(c, d, piece).wait()

    def load_leg(c):
        at = pl.multiple_of(8 * c, 8)
        return pltpu.make_async_copy(
            legendre_ref.at[pl.ds(at, 8)], leg.at[lax.rem(c, 2)], leg_sem.at[c]
        )

    def give(c, h, d):
        to = lax.rem(band + d, bands)
        return pltpu.make_async_remote_copy(
            src_ref=part.at[lax.rem(c, 2), to, pl.ds(run * h, run)],
            dst_ref=other.at[d - 1, c, pl.ds(run * h, run)],
            send_sem=part_sem.at[c, h, d],
            recv_sem=other_sem.at[c, h, d],
            device_id={"band": to},
            device_id_type=MESH,
        )

    for t in range(control.shape[0]):
        load_control(t).start()
    points_own.start()
    greet(["col", "band"])
    for d in range(1, owners):
        points_copy(d).start()

    for copy in small:
        copy.wait()
    lane = lax.broadcasted_iota(jnp.int32, (1, LANES), 1)
    rel = lane - plan_ref[0, 1]
    rel = jnp.where(rel < 0, rel + LANES, rel)
    spare = rel >= LVR
    band_id = plan_ref[0, 0]
    root = root_ref[0]
    for b in range(1, root_ref.shape[0]):
        here = jnp.full(root.shape, band_id, jnp.int32) == b
        root = jnp.where(here, root_ref[b].astype(jnp.float32), root.astype(jnp.float32))
        root = root.astype(jnp.bfloat16)
    levels = root.shape[0]

    for n, (lo, width) in enumerate(lat_tiles(lats)):

        def root_tile(t, carry, n=n, lo=lo, width=width):
            if n == 0:
                load_control(t).wait()
            values = control[t, :, :, lo : lo + width].astype(jnp.float32)
            planes[:, :width] = values.reshape(levels * 16, width)
            for j in range(16):
                plane = planes[pl.ds(j, levels, stride=16), :][:, :width]
                rooted = lax.dot_general(
                    plane.astype(jnp.bfloat16),
                    root,
                    (((0,), (0,)), ((), ())),
                    preferred_element_type=jnp.float32,
                )
                rows_of[pl.ds(j, width, stride=16), :] = rooted
            at = pl.multiple_of(16 * t, 16)
            for k, (first, step, tile) in enumerate(plan):
                if tile != n:
                    continue

                def owner(to, c, k=k, first=first, step=step):
                    start = pl.multiple_of((first - lo + step * to) * 16, 128)
                    extra = rows_of[pl.ds(start + 16 * PACK, 16), :]
                    for g in range(PACK):
                        mine = rows_of[pl.ds(start + 16 * g, 16), :]
                        moved = pltpu.roll(extra, LVR - GROUP * g, 1)
                        value = jnp.where(spare, moved, mine).astype(jnp.bfloat16)
                        sent[k, to, g, pl.ds(at, 16), :] = value
                    return c

                lax.fori_loop(0, owners, owner, 0, unroll=True)
                if k == 0:
                    for d in range(1, owners):
                        piece_copy(t, d).start()
            return carry

        lax.fori_loop(0, control.shape[0], root_tile, 0)
        if n == 0:
            grid_own(0).start()
            grid_send(1)
            for c in range(2):
                load_leg(c).start()
    for d in range(1, owners):
        points_copy(d).wait()
    points_own.wait()

    def wave_row(r, carry):
        sl, rest = r // eighth, lax.rem(r, eighth)
        c, dev = rest // owners, lax.rem(rest, owners)
        value = order_ref[dev * (8 * groups) + 8 * c + sl]
        wave[pl.ds(r, 1), :] = jnp.full((1, LANES), 4 * value, jnp.int32).astype(jnp.float32)
        return carry

    lax.fori_loop(0, waves, wave_row, 0)
    lower, upper = support_ref[0, band_id], support_ref[1, band_id]

    def window_row(n, carry):
        row = jnp.full((1, LANES), filter_ref[band_id, n], jnp.float32)
        at = jnp.full((1, LANES), n, jnp.int32)
        live = (at >= lower) & (at < upper) & (rel < LVR)
        window[pl.ds(n, 1), :] = jnp.where(live, row, 0.0)
        return carry

    lax.fori_loop(0, total, window_row, 0)

    def transform(k, lat, x):
        for p in range(2):
            res = jnp.dot(
                weight[lat, p * waves : (p + 1) * waves, :],
                x,
                preferred_element_type=jnp.float32,
            )
            extra = res[PACK * eighth :]
            for g in range(PACK):
                moved = pltpu.roll(extra, LVR - GROUP * g, 1)
                piece = jnp.where(spare, moved, res[g * eighth : (g + 1) * eighth])
                turned[pl.ds(g * eighth * 16 + p * 8 + lat, eighth, stride=16), :] = piece

    def chunk(k, carry):
        first, step = jnp.int32(0), jnp.int32(0)
        for i, (lo, by, _) in enumerate(plan):
            first = jnp.where(k == i, lo, first)
            step = jnp.where(k == i, by, step)

        def make(lat, c):
            index = first + step * me + lat
            held = lats // owners
            row = points[index // held].astype(jnp.float32)
            column = lax.broadcasted_iota(jnp.int32, row.shape, 1)
            row = jnp.where(column == lax.rem(index, held), row, 0.0)
            count = jnp.sum(row, axis=1, keepdims=True)
            lat_weights(count, wave, lons, weight, lat, 32 if waves % 32 == 0 else 8)
            return c

        lax.fori_loop(0, 8, make, 0)
        @pl.when(k == 0)
        def _():
            for t in range(control.shape[0]):
                for d in range(1, owners):
                    piece_copy(t, d).wait()

        @pl.when(k > 0)
        def _():
            for d in range(1, owners):
                grid_copy(k, d).wait()

        grid_own(k).wait()

        @pl.when(k + 2 < chunks)
        def _():
            grid_send(k + 2)

        @pl.when(k == chunks - 1)
        def _():
            for q in range(1, pace):
                wave_start(0, pace + q)

        def plain(g, c):
            transform(k, g, got[k, :, g].reshape(lons, LANES))
            return c

        lax.fori_loop(0, PACK, plain, 0)
        x = jnp.zeros((lons, LANES), jnp.float32)
        for g in range(PACK):
            moved = got[k, :, g].reshape(lons, LANES).astype(jnp.float32)
            moved = pltpu.roll(moved, LANES - LVR + GROUP * g, 1)
            x = jnp.where((rel >= GROUP * g) & (rel < GROUP * (g + 1)), moved, x)
        transform(k, PACK, x.astype(jnp.bfloat16))
        for c in range(groups):
            for g in range(PACK):
                at = (g * eighth + c * owners) * 16
                rows = turned[at : at + 16 * owners, :].reshape(owners, 16, LANES)
                fourier[c, :, k, g] = rows.astype(jnp.bfloat16)

        @pl.when(k == early - 1)
        def _():
            wave_start(0, pace)

        return carry

    lax.fori_loop(0, chunks, chunk, 0)
    wave_start(0, "late")
    wave_own(0).start()
    for q in range(DEPTH):
        wave_start(1, q)
    wave_own(1).start()

    tiles = [
        [k for k, entry in enumerate(plan) if entry[2] == n]
        for n in range(len(lat_tiles(lats)))
    ]

    def finish(c):
        for h in range(pace):
            for d in range(1, bands):
                give(c, h, d).wait_recv()
            for sl in range(run * h, run * (h + 1)):
                for p in range(2):
                    acc = part[lax.rem(c, 2), band, sl, p].astype(jnp.float32)
                    for d in range(1, bands):
                        acc = acc + other[d - 1, c, sl, p].astype(jnp.float32)
                    out_ref[8 * c + sl, pl.ds(p, degrees, stride=2), :] = acc

    def slot_out(c, sl, halves):
        res = jnp.dot(
            leg_t[sl],
            jnp.concatenate([h.astype(jnp.bfloat16) for h in halves], axis=1),
            preferred_element_type=jnp.float32,
        )
        degree = lax.broadcasted_iota(jnp.int32, (total, LANES), 0)
        order_here = order_ref[me * (8 * groups) + 8 * c + sl]
        keep = jnp.where(degree >= order_here, window[...], 0.0)
        for p in range(2):
            value = (res[:, p * LANES : (p + 1) * LANES] * keep).astype(jnp.bfloat16)
            part[lax.rem(c, 2), :, sl, p] = value.reshape(bands, degrees, LANES)
        if sl % run == run - 1:
            for d in range(1, bands):
                give(c, sl // run, d).start()

    def group(c, carry):
        load_leg(c).wait()
        for sl in range(8):
            leg_t[sl] = leg[lax.rem(c, 2), sl].T

        @pl.when(c + 2 < groups)
        def _():
            load_leg(c + 2).start()

        def arrive(q):
            @pl.when(c == 0)
            def _():
                wave_wait(0, pace + q)
                if q == 0:
                    wave_wait(0, "late")

            @pl.when(c > 0)
            def _():
                wave_wait(c, q)
                if q + DEPTH < pace:
                    wave_start(c, q + DEPTH)

            @pl.when((c > 0) & (c + 1 < groups))
            def _():
                if q + DEPTH >= pace:
                    wave_start(c + 1, q + DEPTH - pace)

        arrive(0)
        wave_own(c).wait()

        @pl.when(c + 2 < groups)
        def _():
            wave_own(c + 2).start()

        @pl.when(c >= 2)
        def _():
            for h in range(pace):
                for d in range(1, bands):
                    give(c - 2, h, d).wait_send()

        for sl in range(PACK):
            if sl and sl % run == 0:
                arrive(sl // run)
            value = [
                owned[c, :, tile[0] : tile[-1] + 1, sl].astype(jnp.float32)
                for tile in tiles
            ]
            value = [v.reshape(-1, 2, 8, LANES) for v in value]
            value = jnp.concatenate(value, axis=0)
            halves = [value[:, p].reshape(lats, LANES) for p in range(2)]
            here = (rel >= GROUP * sl) & (rel < GROUP * (sl + 1))
            for p in range(2):
                moved = pltpu.roll(halves[p], LANES - LVR + GROUP * sl, 1)
                before = last[p] if sl else jnp.zeros((lats, LANES), jnp.float32)
                last[p] = jnp.where(here, moved, before)
            slot_out(c, sl, halves)
        slot_out(c, PACK, [last[0], last[1]])

        @pl.when(c >= 1)
        def _():
            finish(c - 1)

        return carry

    lax.fori_loop(0, groups, group, 0)
    finish(groups - 1)
    for c in range(groups - 2, groups):
        for h in range(pace):
            for d in range(1, bands):
                give(c, h, d).wait_send()


def chain(points, plan, order, band_filter, support, root, control, legendre, owners, bands):
    levels, lon_local, lats = control.shape
    slot_count, _, total = legendre.shape
    waves = order.shape[0]
    chunks, groups = lats // owners // 8, slot_count // 8
    lons, degrees, pace = owners * lon_local, total // bands, 4
    bf16, f32 = jnp.bfloat16, jnp.float32
    any_spec = pl.BlockSpec(memory_space=pl.ANY)
    vmem_spec = pl.BlockSpec(memory_space=pltpu.VMEM)
    dma = pltpu.SemaphoreType.DMA
    return pl.pallas_call(
        chain_kernel,
        in_specs=[any_spec] * 8,
        out_specs=vmem_spec,
        out_shape=pltpu.VMEM((slot_count, 2 * degrees, LANES), f32),
        scratch_shapes=[
            pltpu.SMEM(plan.shape, jnp.int32),
            pltpu.SMEM(order.shape, jnp.int32),
            pltpu.SMEM(band_filter.shape, f32),
            pltpu.SMEM(support.shape, jnp.int32),
            pltpu.VMEM(root.shape, bf16),
            pltpu.VMEM((waves, LANES), f32),
            pltpu.VMEM((total, LANES), f32),
            pltpu.VMEM((owners, 1, lats // owners), jnp.int32),
            pltpu.VMEM((lon_local // 16, levels, 16, lats), bf16),
            pltpu.VMEM((levels * 16, LANES), f32),
            pltpu.VMEM((16 * LANES, LANES), f32),
            pltpu.VMEM((chunks, owners, PACK, lon_local, LANES), bf16),
            pltpu.VMEM((chunks, owners, PACK, lon_local, LANES), bf16),
            pltpu.VMEM((8, 2 * waves, lons), bf16),
            pltpu.VMEM((PACK * waves // 8 * 16, LANES), f32),
            pltpu.VMEM((groups, owners, chunks, PACK, 16, LANES), bf16),
            pltpu.VMEM((groups, owners, chunks, PACK, 16, LANES), bf16),
            pltpu.VMEM((2, 8, lats, total), bf16),
            pltpu.VMEM((8, total, lats), bf16),
            pltpu.VMEM((2, lats, LANES), f32),
            pltpu.VMEM((2, bands, 8, 2, degrees, LANES), bf16),
            pltpu.VMEM((bands - 1, groups, 8, 2, degrees, LANES), bf16),
            dma((owners,)),
            dma((owners,)),
            dma((lon_local // 16,)),
            dma((lon_local // 16, owners)),
            dma((lon_local // 16, owners)),
            dma((5,)),
            dma((chunks, owners)),
            dma((chunks, owners)),
            dma((chunks,)),
            dma((groups, owners, pace + 1)),
            dma((groups, owners, pace + 1)),
            dma((groups,)),
            dma((groups,)),
            dma((groups, pace, bands)),
            dma((groups, pace, bands)),
        ],
        compiler_params=pltpu.CompilerParams(
            collective_id=0, has_side_effects=True, vmem_limit_bytes=VMEM_LIMIT
        ),
        cost_estimate=pl.CostEstimate(flops=8 * 10**9, bytes_accessed=40 * 10**6, transcendentals=0),
        name="chain",
    )(points, plan, order, band_filter, support, root, control, legendre)


def per_device_fused(
    control, vertical_root, legendre, band_filter, row_plan, wave_order, lat_points, support
):
    bands = lax.axis_size("band")
    result = chain(
        lat_points[None, :],
        row_plan,
        wave_order,
        band_filter,
        support.T,
        vertical_root,
        control[0].transpose(2, 0, 1),
        legendre,
        lax.axis_size("col"),
        bands,
    )
    slot_count, _, total = legendre.shape
    return result.reshape(slot_count, total // bands, 2, LANES)


def per_device(control, vertical_root, legendre, *rest):
    owners, bands = lax.axis_size("col"), lax.axis_size("band")
    _, lon_local, lats, _ = control.shape
    slot_count, _, total = legendre.shape
    chunks = lats // owners // 8
    fits = (
        vertical_root.shape[2] == LANES
        and all(width % (8 * owners) == 0 for _, width in lat_tiles(lats))
        and lats % (8 * owners) == 0
        and lon_local % 16 == 0
        and (owners * lon_local) % LANES == 0
        and chunks >= 3
        and slot_count % 8 == 0
        and slot_count >= 24
        and (slot_count // 8 * owners) % 8 == 0
        and total % bands == 0
        and (total // bands) % 16 == 0
        and bands > 1
    )
    body = per_device_fused if fits else per_device_plain
    return body(control, vertical_root, legendre, *rest)


def solution(mesh):
    in_specs = (
        P("band", "col", None, None),
        P(),
        P("col", None, None),
        P(),
        P("band", None),
        P(),
        P("col"),
        P(),
    )
    out_specs = P("col", "band", None, None)
    return jax.shard_map(
        per_device, mesh=mesh, in_specs=in_specs, out_specs=out_specs, check_vma=False
    )
```

```python
import functools
import math

import jax
import jax.numpy as jnp
from jax import lax
from jax.experimental import pallas as pl
from jax.experimental.pallas import tpu as pltpu
from jax.sharding import PartitionSpec as P

LVR = 112
CHUNKS = (2, 2, 1)
LANES = 128
GROUP = 16
DEPTH = 2
PACE = 4
VMEM_LIMIT = 58 * 2**20
PACK = LVR // GROUP
MESH = pl.DeviceIdType.MESH


def sine(theta):
    square = theta * theta
    value = -1.0 / 39916800.0 * square + 1.0 / 362880.0
    value = value * square - 1.0 / 5040.0
    value = value * square + 1.0 / 120.0
    value = value * square - 1.0 / 6.0
    value = value * square + 1.0
    return value * theta


def weights_kernel(points_ref, wave_ref, *out_refs):
    count = jnp.full((1, 1), points_ref[pl.program_id(0)], jnp.int32).astype(jnp.float32)
    lons = out_refs[0].shape[2]
    lanes = 128
    lon = lax.broadcasted_iota(jnp.int32, (1, lons), 1).astype(jnp.float32)
    full = 4.0 * count
    inverse = 1.0 / full
    unit = (2.0 * math.pi) * inverse
    scale = jnp.where(lon < count, lax.rsqrt(count), 0.0)
    nearest = 1.5 * 2.0**23
    first = 0
    for out_ref in out_refs:
        half = out_ref.shape[1] // 2
        tile = 8 if half % 16 else 16

        def rows(k, carry, out_ref=out_ref, first=first, tile=tile, half=half):
            at = pl.multiple_of(k * tile, tile)
            turns = wave_ref[pl.ds(first + at, tile), :] * lon[:, :lanes]
            whole = (turns * inverse + nearest) - nearest
            rest = turns - whole * full
            cos = sine((count - jnp.abs(rest)) * unit)
            away = jnp.abs(rest - count)
            sin = sine((count - jnp.minimum(away, full - away)) * unit)
            middle = lanes // 2
            cos_half = jnp.broadcast_to(cos[:, middle : middle + 1], cos.shape)
            sin_half = jnp.broadcast_to(sin[:, middle : middle + 1], sin.shape)
            cos_step = cos_half * cos_half - sin_half * sin_half
            sin_step = 2.0 * (cos_half * sin_half)
            for lo in range(0, lons, lanes):
                if lo:
                    cos, sin = (
                        cos * cos_step - sin * sin_step,
                        sin * cos_step + cos * sin_step,
                    )
                part = scale[:, lo : lo + lanes]
                out_ref[0, pl.ds(at, tile), lo : lo + lanes] = (cos * part).astype(
                    jnp.bfloat16
                )
                out_ref[0, pl.ds(half + at, tile), lo : lo + lanes] = (-sin * part).astype(
                    jnp.bfloat16
                )
            return carry

        lax.fori_loop(0, half // tile, rows, 0)
        first += half


def dft_weights(points, chunks, lon_count):
    lats = points.shape[0]
    shapes = [(lats, 2 * waves.size, lon_count) for waves in chunks]
    wave = jnp.concatenate([waves.reshape(-1) for waves in chunks])
    wave = 4.0 * wave.astype(jnp.float32)[:, None]
    return pl.pallas_call(
        weights_kernel,
        grid_spec=pltpu.PrefetchScalarGridSpec(
            num_scalar_prefetch=1,
            grid=(lats,),
            in_specs=[pl.BlockSpec(wave.shape, lambda i, p: (0, 0))],
            out_specs=[pl.BlockSpec((1,) + sh[1:], lambda i, p: (i, 0, 0)) for sh in shapes],
        ),
        out_shape=[jax.ShapeDtypeStruct(sh, jnp.bfloat16) for sh in shapes],
        cost_estimate=pl.CostEstimate(
            flops=20 * lats * wave.shape[0] * lon_count,
            bytes_accessed=4 * lats * wave.shape[0] * lon_count,
            transcendentals=0,
        ),
        name="weights",
    )(points, wave)


def dft_kernel(weight_ref, grid_ref, out_ref):
    lons = grid_ref.shape[0] * grid_ref.shape[2]
    owners, _, parts, slots, levels = out_ref.shape
    half = owners * slots
    for i in range(grid_ref.shape[1]):
        column = grid_ref[:, i].reshape(lons, levels)
        result = jnp.dot(weight_ref[i], column, preferred_element_type=jnp.float32)
        for p in range(parts):
            piece = result[p * half : (p + 1) * half].reshape(owners, slots, levels)
            out_ref[:, i, p] = piece.astype(jnp.bfloat16)


def dft(weights, grid_field, owners):
    lats, cols, lons = weights.shape
    ranks, _, lon_local, levels = grid_field.shape
    slots = cols // (2 * owners)
    block = max(d for d in range(1, 9) if lats % d == 0)
    return pl.pallas_call(
        dft_kernel,
        grid=(lats // block,),
        in_specs=[
            pl.BlockSpec((block, cols, lons), lambda i: (i, 0, 0)),
            pl.BlockSpec((ranks, block, lon_local, levels), lambda i: (0, i, 0, 0)),
        ],
        out_specs=pl.BlockSpec((owners, block, 2, slots, levels), lambda i: (0, i, 0, 0, 0)),
        out_shape=jax.ShapeDtypeStruct((owners, lats, 2, slots, levels), jnp.bfloat16),
        cost_estimate=pl.CostEstimate(
            flops=2 * lats * cols * lons * levels,
            bytes_accessed=2 * lats * (cols * lons + (cols + lons) * levels),
            transcendentals=0,
        ),
        name="dft",
    )(weights, grid_field)


def per_device_plain(
    control, vertical_root, legendre, band_filter, row_plan, wave_order, lat_points, support
):
    owners = lax.axis_size("col")
    band_id = row_plan[0, 0]
    level_start = row_plan[0, 1]
    root_band = lax.dynamic_index_in_dim(vertical_root, band_id, 0, keepdims=False)
    level = jnp.arange(root_band.shape[1], dtype=jnp.int32)
    inside = (level >= level_start) & (level < level_start + LVR)
    root_block = jnp.where(inside[None, :], root_band, jnp.zeros_like(root_band))
    columns = control[0]
    lon_local, lat_count, _ = columns.shape
    rooted = jnp.einsum(
        "jik,kl->ijl", columns, root_block, preferred_element_type=jnp.float32
    ).astype(jnp.bfloat16)
    rooted = rooted.reshape(owners, lat_count // owners, lon_local, -1)
    grid_field = lax.all_to_all(rooted, "col", split_axis=0, concat_axis=0, tiled=True)
    lon_count = lon_local * owners
    lat_local = lat_count // owners

    slot_count = legendre.shape[0]
    degree_count = legendre.shape[2]
    ends = [slot_count * sum(CHUNKS[: c + 1]) // sum(CHUNKS) for c in range(len(CHUNKS))]
    spans = list(zip([0] + ends[:-1], ends))
    waves = wave_order.reshape(owners, slot_count)
    owned_waves = lax.dynamic_index_in_dim(waves, lax.axis_index("col"), 0, keepdims=False)
    degree = jnp.arange(degree_count, dtype=jnp.int32)
    bounds = lax.dynamic_index_in_dim(support, band_id, 0, keepdims=False)
    filter_row = lax.dynamic_index_in_dim(band_filter, band_id, 0, keepdims=False)
    window = filter_row * ((degree >= bounds[0]) & (degree < bounds[1])).astype(jnp.float32)

    weights = dft_weights(lat_points, [waves[:, lo:hi] for lo, hi in spans], lon_count)
    outputs = []
    fourier = dft(weights[0], grid_field, owners)
    for c, (lo, hi) in enumerate(spans):
        owned = lax.all_to_all(fourier, "col", split_axis=0, concat_axis=0, tiled=True)
        if c + 1 < len(spans):
            fourier = dft(weights[c + 1], grid_field, owners)
        if c:
            fourier, owned, _ = lax.optimization_barrier((fourier, owned, contribution))
        else:
            fourier, owned = lax.optimization_barrier((fourier, owned))
        owned = owned.reshape(lat_count, 2, hi - lo, owned.shape[4])
        spectral = jnp.einsum(
            "xpsl,sxn->snpl",
            owned,
            legendre[lo:hi],
            preferred_element_type=jnp.float32,
        )
        spectral_weight = (degree[None, :] >= owned_waves[lo:hi][:, None]).astype(
            jnp.float32
        ) * window[None, :]
        contribution = (spectral * spectral_weight[:, :, None, None]).astype(jnp.bfloat16)
        if c:
            contribution, outputs[-1] = lax.optimization_barrier((contribution, outputs[-1]))
        outputs.append(
            lax.psum_scatter(contribution, "band", scatter_dimension=1, tiled=True)
        )
    return jnp.concatenate(outputs, axis=0).astype(jnp.float32)


def greet(axes):
    barrier = pltpu.get_barrier_semaphore()
    total = 0
    for axis in axes:
        size, me = lax.axis_size(axis), lax.axis_index(axis)
        for d in range(1, size):
            pl.semaphore_signal(
                barrier,
                inc=1,
                device_id={axis: lax.rem(me + d, size)},
                device_id_type=MESH,
            )
        total += size - 1
    return barrier, total


def lat_weights(count, wave_ref, lons, out_ref, index, tile):
    full = 4.0 * count
    inverse = 1.0 / full
    unit = (2.0 * math.pi) * inverse
    lon = lax.broadcasted_iota(jnp.int32, (1, lons), 1).astype(jnp.float32)
    scale = jnp.where(lon < count, lax.rsqrt(count), 0.0)
    nearest = 1.5 * 2.0**23
    half = wave_ref.shape[0]

    def rows(k, carry):
        at = pl.multiple_of(k * tile, tile)
        turns = wave_ref[pl.ds(at, tile), :] * lon[:, :LANES]
        whole = (turns * inverse + nearest) - nearest
        rest = turns - whole * full
        cos = sine((count - jnp.abs(rest)) * unit)
        away = jnp.abs(rest - count)
        sin = sine((jnp.minimum(away, full - away) - count) * unit)
        middle = LANES // 2
        cos_half = jnp.broadcast_to(cos[:, middle : middle + 1], cos.shape)
        sin_half = jnp.broadcast_to(sin[:, middle : middle + 1], sin.shape)
        cos_step = cos_half * cos_half - sin_half * sin_half
        sin_step = 2.0 * (cos_half * sin_half)
        for lo in range(0, lons, LANES):
            if lo:
                cos, sin = (
                    cos * cos_step - sin * sin_step,
                    sin * cos_step + cos * sin_step,
                )
            part = scale[:, lo : lo + LANES]
            out_ref[index, pl.ds(at, tile), lo : lo + LANES] = (cos * part).astype(
                jnp.bfloat16
            )
            out_ref[index, pl.ds(half + at, tile), lo : lo + LANES] = (
                sin * part
            ).astype(jnp.bfloat16)
        return carry

    lax.fori_loop(0, half // tile, rows, 0)


def lat_tiles(lats):
    return [(lo, min(LANES, lats - lo)) for lo in range(0, lats, LANES)]


def lat_chunks(lats, owners):
    out = []
    for n, (lo, width) in enumerate(lat_tiles(lats)):
        step = width // owners
        out += [(lo + at, step, n) for at in range(0, step, 8)]
    return out


def chain_kernel(
    points_ref,
    plan_any,
    order_any,
    filter_any,
    support_any,
    root_any,
    control_ref,
    legendre_ref,
    out_ref,
    plan_ref,
    order_ref,
    filter_ref,
    support_ref,
    root_ref,
    wave,
    window,
    points,
    control,
    planes,
    rows_of,
    sent,
    got,
    weight,
    turned,
    fourier,
    owned,
    leg,
    leg_t,
    last,
    part,
    other,
    points_sem,
    points_got_sem,
    control_sem,
    piece_sem,
    piece_got_sem,
    small_sem,
    send_sem,
    recv_sem,
    own_sem,
    send2_sem,
    recv2_sem,
    own2_sem,
    leg_sem,
    part_sem,
    other_sem,
):
    chunks, owners, _, lon_local, _ = sent.shape
    groups = fourier.shape[0]
    bands, _, _, degrees, _ = part.shape[1:]
    lons = owners * lon_local
    lats = owners * chunks * 8
    waves, total = wave.shape[0], window.shape[0]
    eighth = waves // 8
    early = chunks - 1
    plan = lat_chunks(lats, owners)
    pace = part_sem.shape[1]
    run = 8 // pace
    parts = -(-PACK // run)
    me, band = lax.axis_index("col"), lax.axis_index("band")

    small = [
        pltpu.make_async_copy(src, dst, small_sem.at[i])
        for i, (src, dst) in enumerate(
            [
                (plan_any, plan_ref),
                (root_any, root_ref),
                (order_any, order_ref),
                (filter_any, filter_ref),
                (support_any, support_ref),
            ]
        )
    ]
    barrier, peers = greet(["col", "band"])
    for copy in small:
        copy.start()

    def load_control(t):
        at = pl.multiple_of(16 * t, 16)
        return pltpu.make_async_copy(
            control_ref.at[:, pl.ds(at, 16), :], control.at[t], control_sem.at[t]
        )

    def across(src, dst, send, recv, to):
        return pltpu.make_async_remote_copy(
            src_ref=src,
            dst_ref=dst,
            send_sem=send,
            recv_sem=recv,
            device_id={"col": to},
            device_id_type=MESH,
        )

    def grid_copy(k, d):
        to = lax.rem(me + d, owners)
        return across(
            sent.at[k, to], got.at[k, me], send_sem.at[k, d], recv_sem.at[k, d], to
        )

    def points_copy(d):
        to = lax.rem(me + d, owners)
        return across(
            points_ref, points.at[me], points_sem.at[d], points_got_sem.at[d], to
        )

    points_own = pltpu.make_async_copy(points_ref, points.at[me], points_sem.at[0])

    def piece_copy(t, d):
        to = lax.rem(me + d, owners)
        rows = pl.ds(pl.multiple_of(16 * t, 16), 16)
        return across(
            sent.at[0, to, :, rows],
            got.at[0, me, :, rows],
            piece_sem.at[t, d],
            piece_got_sem.at[t, d],
            to,
        )

    def grid_own(k):
        return pltpu.make_async_copy(sent.at[k, me], got.at[k, me], own_sem.at[k])

    def grid_send(k):
        for d in range(1, owners):
            grid_copy(k, d).start()
        grid_own(k).start()

    def view(ref, c, dev, piece):
        if piece == "late":
            return ref.at[c, dev, :, pl.ds(early, 1)]
        first = piece % parts * run
        tiles = pl.ds(first, min(run, PACK - first))
        if piece >= parts:
            return ref.at[c, dev, tiles, pl.ds(0, early)]
        return ref.at[c, dev, tiles]

    def wave_copy(c, d, piece):
        to = lax.rem(me + d, owners)
        e = parts if piece == "late" else piece % parts
        return across(
            view(fourier, c, to, piece),
            view(owned, c, me, piece),
            send2_sem.at[c, d, e],
            recv2_sem.at[c, d, e],
            to,
        )

    def wave_own(c):
        return pltpu.make_async_copy(fourier.at[c, me], owned.at[c, me], own2_sem.at[c])

    def wave_start(c, piece):
        for d in range(1, owners):
            wave_copy(c, d, piece).start()

    def wave_wait(c, piece):
        for d in range(1, owners):
            wave_copy(c, d, piece).wait()

    def load_leg(c):
        at = pl.multiple_of(8 * c, 8)
        return pltpu.make_async_copy(
            legendre_ref.at[pl.ds(at, 8)], leg.at[lax.rem(c, 2)], leg_sem.at[c]
        )

    def give(c, h, d):
        to = lax.rem(band + d, bands)
        return pltpu.make_async_remote_copy(
            src_ref=part.at[lax.rem(c, 2), to, pl.ds(run * h, run)],
            dst_ref=other.at[d - 1, c, pl.ds(run * h, run)],
            send_sem=part_sem.at[c, h, d],
            recv_sem=other_sem.at[c, h, d],
            device_id={"band": to},
            device_id_type=MESH,
        )

    lon_tiles = control.shape[0]
    ahead = min(2, lon_tiles)
    for t in range(ahead):
        load_control(t).start()
    points_own.start()
    for copy in small:
        copy.wait()
    lane = lax.broadcasted_iota(jnp.int32, (1, LANES), 1)
    rel = lane - plan_ref[0, 1]
    rel = jnp.where(rel < 0, rel + LANES, rel)
    spare = rel >= LVR
    band_id = plan_ref[0, 0]
    root = root_ref[0]
    for b in range(1, root_ref.shape[0]):
        here = jnp.full(root.shape, band_id, jnp.int32) == b
        root = jnp.where(here, root_ref[b].astype(jnp.float32), root.astype(jnp.float32))
        root = root.astype(jnp.bfloat16)
    levels = root.shape[0]

    for n, (lo, width) in enumerate(lat_tiles(lats)):

        def root_tile(t, carry, n=n, lo=lo, width=width):
            if n == 0:
                load_control(t).wait()

                @pl.when(t + ahead < lon_tiles)
                def _():
                    load_control(t + ahead).start()

            values = control[t, :, :, lo : lo + width].astype(jnp.float32)
            planes[:, :width] = values.reshape(levels * 16, width)
            for j in range(16):
                plane = planes[pl.ds(j, levels, stride=16), :][:, :width]
                rooted = lax.dot_general(
                    plane.astype(jnp.bfloat16),
                    root,
                    (((0,), (0,)), ((), ())),
                    preferred_element_type=jnp.float32,
                )
                rows_of[pl.ds(j, width, stride=16), :] = rooted
            at = pl.multiple_of(16 * t, 16)
            for k, (first, step, tile) in enumerate(plan):
                if tile != n:
                    continue

                def owner(to, c, k=k, first=first, step=step):
                    start = pl.multiple_of((first - lo + step * to) * 16, 128)
                    extra = rows_of[pl.ds(start + 16 * PACK, 16), :]
                    for g in range(PACK):
                        mine = rows_of[pl.ds(start + 16 * g, 16), :]
                        moved = pltpu.roll(extra, LVR - GROUP * g, 1)
                        value = jnp.where(spare, moved, mine).astype(jnp.bfloat16)
                        sent[k, to, g, pl.ds(at, 16), :] = value
                    return c

                lax.fori_loop(0, owners, owner, 0, unroll=True)
                if k == 0:

                    @pl.when(t == 0)
                    def _():
                        pl.semaphore_wait(barrier, peers)
                        for d in range(1, owners):
                            points_copy(d).start()

                    for d in range(1, owners):
                        piece_copy(t, d).start()
            return carry

        lax.fori_loop(0, lon_tiles, root_tile, 0)
        if n == 0:
            grid_own(0).start()
            grid_send(1)
            for c in range(2):
                load_leg(c).start()
    for d in range(1, owners):
        points_copy(d).wait()
    points_own.wait()

    def wave_row(r, carry):
        sl, rest = r // eighth, lax.rem(r, eighth)
        c, dev = rest // owners, lax.rem(rest, owners)
        value = order_ref[dev * (8 * groups) + 8 * c + sl]
        wave[pl.ds(r, 1), :] = jnp.full((1, LANES), 4 * value, jnp.int32).astype(jnp.float32)
        return carry

    lax.fori_loop(0, waves, wave_row, 0)
    lower, upper = support_ref[0, band_id], support_ref[1, band_id]

    def window_row(n, carry):
        row = jnp.full((1, LANES), filter_ref[band_id, n], jnp.float32)
        at = jnp.full((1, LANES), n, jnp.int32)
        live = (at >= lower) & (at < upper) & (rel < LVR)
        window[pl.ds(n, 1), :] = jnp.where(live, row, 0.0)
        return carry

    lax.fori_loop(0, total, window_row, 0)

    def transform(k, lat, x):
        for p in range(2):
            res = jnp.dot(
                weight[lat, p * waves : (p + 1) * waves, :],
                x,
                preferred_element_type=jnp.float32,
            )
            extra = res[PACK * eighth :]
            for g in range(PACK):
                moved = pltpu.roll(extra, LVR - GROUP * g, 1)
                piece = jnp.where(spare, moved, res[g * eighth : (g + 1) * eighth])
                turned[pl.ds(g * eighth * 16 + p * 8 + lat, eighth, stride=16), :] = piece

    def chunk(k, carry):
        first, step = jnp.int32(0), jnp.int32(0)
        for i, (lo, by, _) in enumerate(plan):
            first = jnp.where(k == i, lo, first)
            step = jnp.where(k == i, by, step)

        def make(lat, c):
            index = first + step * me + lat
            held = lats // owners
            row = points[index // held].astype(jnp.float32)
            column = lax.broadcasted_iota(jnp.int32, row.shape, 1)
            row = jnp.where(column == lax.rem(index, held), row, 0.0)
            count = jnp.sum(row, axis=1, keepdims=True)
            lat_weights(count, wave, lons, weight, lat, 32 if waves % 32 == 0 else 8)
            return c

        lax.fori_loop(0, 8, make, 0)
        @pl.when(k == 0)
        def _():
            for t in range(control.shape[0]):
                for d in range(1, owners):
                    piece_copy(t, d).wait()

        @pl.when(k > 0)
        def _():
            for d in range(1, owners):
                grid_copy(k, d).wait()

        grid_own(k).wait()

        @pl.when(k + 2 < chunks)
        def _():
            grid_send(k + 2)

        @pl.when(k == chunks - 1)
        def _():
            for q in range(1, parts):
                wave_start(0, parts + q)

        def plain(g, c):
            transform(k, g, got[k, :, g].reshape(lons, LANES))
            return c

        lax.fori_loop(0, PACK, plain, 0)
        x = jnp.zeros((lons, LANES), jnp.float32)
        for g in range(PACK):
            moved = got[k, :, g].reshape(lons, LANES).astype(jnp.float32)
            moved = pltpu.roll(moved, LANES - LVR + GROUP * g, 1)
            x = jnp.where((rel >= GROUP * g) & (rel < GROUP * (g + 1)), moved, x)
        transform(k, PACK, x.astype(jnp.bfloat16))
        for c in range(groups):
            for g in range(PACK):
                at = (g * eighth + c * owners) * 16
                rows = turned[at : at + 16 * owners, :].reshape(owners, 16, LANES)
                fourier[c, :, g, k] = rows.astype(jnp.bfloat16)

        @pl.when(k == early - 1)
        def _():
            wave_start(0, parts)

        return carry

    lax.fori_loop(0, chunks, chunk, 0)
    wave_start(0, "late")
    wave_own(0).start()
    for q in range(DEPTH):
        wave_start(1, q)
    wave_own(1).start()

    tiles = [
        [k for k, entry in enumerate(plan) if entry[2] == n]
        for n in range(len(lat_tiles(lats)))
    ]

    def finish(c):
        for h in range(pace):
            for d in range(1, bands):
                give(c, h, d).wait_recv()
            for sl in range(run * h, run * (h + 1)):
                for p in range(2):
                    acc = part[lax.rem(c, 2), band, sl, p].astype(jnp.float32)
                    for d in range(1, bands):
                        acc = acc + other[d - 1, c, sl, p].astype(jnp.float32)
                    out_ref[8 * c + sl, pl.ds(p, degrees, stride=2), :] = acc

    def slot_out(c, sl, halves):
        res = jnp.dot(
            leg_t[sl],
            jnp.concatenate([h.astype(jnp.bfloat16) for h in halves], axis=1),
            preferred_element_type=jnp.float32,
        )
        degree = lax.broadcasted_iota(jnp.int32, (total, LANES), 0)
        order_here = order_ref[me * (8 * groups) + 8 * c + sl]
        keep = jnp.where(degree >= order_here, window[...], 0.0)
        for p in range(2):
            value = (res[:, p * LANES : (p + 1) * LANES] * keep).astype(jnp.bfloat16)
            part[lax.rem(c, 2), :, sl, p] = value.reshape(bands, degrees, LANES)
        if sl % run == run - 1:
            for d in range(1, bands):
                give(c, sl // run, d).start()

    def group(c, carry):
        load_leg(c).wait()
        for sl in range(8):
            leg_t[sl] = leg[lax.rem(c, 2), sl].T

        @pl.when(c + 2 < groups)
        def _():
            load_leg(c + 2).start()

        def arrive(q):
            @pl.when(c == 0)
            def _():
                wave_wait(0, parts + q)
                if q == 0:
                    wave_wait(0, "late")

            @pl.when(c > 0)
            def _():
                wave_wait(c, q)
                if q + DEPTH < parts:
                    wave_start(c, q + DEPTH)

            @pl.when((c > 0) & (c + 1 < groups))
            def _():
                if q + DEPTH >= parts:
                    wave_start(c + 1, q + DEPTH - parts)

        arrive(0)
        wave_own(c).wait()

        @pl.when(c + 2 < groups)
        def _():
            wave_own(c + 2).start()

        @pl.when(c >= 2)
        def _():
            for h in range(pace):
                for d in range(1, bands):
                    give(c - 2, h, d).wait_send()

        for sl in range(PACK):
            if sl and sl % run == 0:
                arrive(sl // run)
            value = [
                owned[c, :, sl, tile[0] : tile[-1] + 1].astype(jnp.float32)
                for tile in tiles
            ]
            value = [v.reshape(-1, 2, 8, LANES) for v in value]
            value = jnp.concatenate(value, axis=0)
            halves = [value[:, p].reshape(lats, LANES) for p in range(2)]
            here = (rel >= GROUP * sl) & (rel < GROUP * (sl + 1))
            for p in range(2):
                moved = pltpu.roll(halves[p], LANES - LVR + GROUP * sl, 1)
                before = last[p] if sl else jnp.zeros((lats, LANES), jnp.float32)
                last[p] = jnp.where(here, moved, before)
            slot_out(c, sl, halves)
        slot_out(c, PACK, [last[0], last[1]])

        @pl.when(c >= 1)
        def _():
            finish(c - 1)

        return carry

    lax.fori_loop(0, groups, group, 0)
    finish(groups - 1)
    for c in range(groups - 2, groups):
        for h in range(pace):
            for d in range(1, bands):
                give(c, h, d).wait_send()


def chain(points, plan, order, band_filter, support, root, control, legendre, owners, bands):
    levels, lon_local, lats = control.shape
    slot_count, _, total = legendre.shape
    waves = order.shape[0]
    chunks, groups = lats // owners // 8, slot_count // 8
    lons, degrees, pace = owners * lon_local, total // bands, PACE
    bf16, f32 = jnp.bfloat16, jnp.float32
    any_spec = pl.BlockSpec(memory_space=pl.ANY)
    vmem_spec = pl.BlockSpec(memory_space=pltpu.VMEM)
    dma = pltpu.SemaphoreType.DMA
    return pl.pallas_call(
        chain_kernel,
        in_specs=[any_spec] * 8,
        out_specs=vmem_spec,
        out_shape=pltpu.VMEM((slot_count, 2 * degrees, LANES), f32),
        scratch_shapes=[
            pltpu.SMEM(plan.shape, jnp.int32),
            pltpu.SMEM(order.shape, jnp.int32),
            pltpu.SMEM(band_filter.shape, f32),
            pltpu.SMEM(support.shape, jnp.int32),
            pltpu.VMEM(root.shape, bf16),
            pltpu.VMEM((waves, LANES), f32),
            pltpu.VMEM((total, LANES), f32),
            pltpu.VMEM((owners, 1, lats // owners), jnp.int32),
            pltpu.VMEM((lon_local // 16, levels, 16, lats), bf16),
            pltpu.VMEM((levels * 16, LANES), f32),
            pltpu.VMEM((16 * LANES, LANES), f32),
            pltpu.VMEM((chunks, owners, PACK, lon_local, LANES), bf16),
            pltpu.VMEM((chunks, owners, PACK, lon_local, LANES), bf16),
            pltpu.VMEM((8, 2 * waves, lons), bf16),
            pltpu.VMEM((PACK * waves // 8 * 16, LANES), f32),
            pltpu.VMEM((groups, owners, PACK, chunks, 16, LANES), bf16),
            pltpu.VMEM((groups, owners, PACK, chunks, 16, LANES), bf16),
            pltpu.VMEM((2, 8, lats, total), bf16),
            pltpu.VMEM((8, total, lats), bf16),
            pltpu.VMEM((2, lats, LANES), f32),
            pltpu.VMEM((2, bands, 8, 2, degrees, LANES), bf16),
            pltpu.VMEM((bands - 1, groups, 8, 2, degrees, LANES), bf16),
            dma((owners,)),
            dma((owners,)),
            dma((lon_local // 16,)),
            dma((lon_local // 16, owners)),
            dma((lon_local // 16, owners)),
            dma((5,)),
            dma((chunks, owners)),
            dma((chunks, owners)),
            dma((chunks,)),
            dma((groups, owners, pace + 1)),
            dma((groups, owners, pace + 1)),
            dma((groups,)),
            dma((groups,)),
            dma((groups, pace, bands)),
            dma((groups, pace, bands)),
        ],
        compiler_params=pltpu.CompilerParams(
            collective_id=0, has_side_effects=True, vmem_limit_bytes=VMEM_LIMIT
        ),
        cost_estimate=pl.CostEstimate(flops=8 * 10**9, bytes_accessed=40 * 10**6, transcendentals=0),
        name="chain",
    )(points, plan, order, band_filter, support, root, control, legendre)


def per_device_fused(
    control, vertical_root, legendre, band_filter, row_plan, wave_order, lat_points, support
):
    bands = lax.axis_size("band")
    result = chain(
        lat_points[None, :],
        row_plan,
        wave_order,
        band_filter,
        support.T,
        vertical_root,
        control[0].transpose(2, 0, 1),
        legendre,
        lax.axis_size("col"),
        bands,
    )
    slot_count, _, total = legendre.shape
    return result.reshape(slot_count, total // bands, 2, LANES)


def per_device(control, vertical_root, legendre, *rest):
    owners, bands = lax.axis_size("col"), lax.axis_size("band")
    _, lon_local, lats, _ = control.shape
    slot_count, _, total = legendre.shape
    chunks = lats // owners // 8
    fits = (
        vertical_root.shape[2] == LANES
        and all(width % (8 * owners) == 0 for _, width in lat_tiles(lats))
        and lats % (8 * owners) == 0
        and lon_local % 16 == 0
        and (owners * lon_local) % LANES == 0
        and chunks >= 3
        and slot_count % 8 == 0
        and slot_count >= 24
        and (slot_count // 8 * owners) % 8 == 0
        and total % bands == 0
        and (total // bands) % 16 == 0
        and bands > 1
    )
    body = per_device_fused if fits else per_device_plain
    return body(control, vertical_root, legendre, *rest)


def solution(mesh):
    in_specs = (
        P("band", "col", None, None),
        P(),
        P("col", None, None),
        P(),
        P("band", None),
        P(),
        P("col"),
        P(),
    )
    out_specs = P("col", "band", None, None)
    return jax.shard_map(
        per_device, mesh=mesh, in_specs=in_specs, out_specs=out_specs, check_vma=False
    )
```
